128 devices in a mesh: ch: 16 (over z, y), sx: 4 (over x_lo, core), sy: 2 (over x_hi).
Axes of the slice: x: 4 (x_hi: 2, x_lo: 2; x = x_hi * 2 + x_lo), y: 4, z: 4, core: 2. Of those that a mesh axis runs over, the one named last changes fastest.
Arguments:
- inputs: bfloat16 [768, 16, 4, 64], P('ch', 'sx', 'sy'), may hold values from -6 to 6
- pre_act: bfloat16 [768, 16, 4, 64], P('ch', 'sx', 'sy'), may hold values from -6 to 6
- out_grad: bfloat16 [768, 16, 4, 64], P('ch', 'sx', 'sy'), may hold values from -6 to 6
- weight_one: bfloat16 [27, 768, 768], P(None, 'ch'), may hold values from -0.0390625 to 0.0390625
- weight_two: bfloat16 [27, 768, 768], P(None, 'ch'), may hold values from -0.0390625 to 0.0390625
Outputs:
- input_grad: bfloat16 [768, 16, 4, 64], P('ch', 'sx', 'sy')
- filter_one_grad: float32 [27, 768, 768], P(None, 'ch')
- filter_two_grad: float32 [27, 768, 768], P(None, 'ch')
The draws below stay inside these ranges and needn't reach their ends.
All inputs are finite; a program needn't handle non-finite values.
Results may differ from the reference program's by a relative error of at most 0.0049.
Values may be sent and summed in bfloat16 or wider, within the bound.
No kernel may reach another device: no remote copies, remote signals or barrier semaphores. Data moves between devices by JAX's collectives and lax.ppermute only.
A program may use at most 192 MiB of HBM per device.

```python
import math
import jax
import jax.numpy as jnp
from jax import lax

C = 768
NX = 16
NY = 4
NZ = 64


def block_levels(stream_key, extent, pieces, smallest, top_value):
    gain, own = 1.0, jax.random.fold_in(stream_key, 6)
    for dim, parts in pieces:
        steps = jnp.exp(jax.random.uniform(jax.random.fold_in(own, dim), (parts,), jnp.float32, smallest / len(pieces), top_value / len(pieces)))
        gain = gain * jnp.repeat(steps, extent[dim] // parts).reshape([-1 if axis == dim else 1 for axis in range(len(extent))])
    return gain


def scatter_about(own_key, extent, width, bound, shards=(), held_as=jnp.bfloat16):
    values = width * jax.random.normal(own_key, extent, jnp.float32)
    if shards:
        values = values * block_levels(own_key, extent, shards, -0.22, 0.18)
    return jnp.clip(values, -bound, bound).astype(held_as)


def setup_inputs(seed: int = 0) -> dict:
    seeds = jax.random.split(jax.random.key(seed), 6)
    return {
        "inputs": scatter_about(seeds[0], (C, NX, NY, NZ), 1.0, 6.0, ((0, 16), (1, 4), (2, 2))),
        "pre_act": scatter_about(seeds[1], (C, NX, NY, NZ), 1.0, 6.0, ((0, 16), (1, 4), (2, 2))),
        "out_grad": scatter_about(seeds[2], (C, NX, NY, NZ), 1.0, 6.0, ((0, 16), (1, 4), (2, 2))),
        "weight_one": scatter_about(seeds[3], (27, C, C), (27 * C) ** -0.5, 0.0390625, ((1, 16),)),
        "weight_two": scatter_about(seeds[4], (27, C, C), (27 * C) ** -0.5, 0.0390625, ((1, 16),)),
    }


def window(padded, offset, mirror):
    first = offset // 9
    second = offset // 3 % 3
    third = offset % 3
    if mirror:
        first, second, third = (2 - first, 2 - second, 2 - third)
    part = padded[:, first:first + NX, second:second + NY, third:third + NZ]
    return part.reshape(C, NX * NY * NZ)

def pad_all(array):
    return jnp.pad(array, ((0, 0), (1, 1), (1, 1), (1, 1)))

def contract_positions(left, right):
    return lax.dot_general(left, right, (((1,), (1,)), ((), ())), preferred_element_type=jnp.float32)

def reference(inputs, pre_act, out_grad, weight_one, weight_two):
    positions = NX * NY * NZ
    inputs_pad = pad_all(inputs)
    grad_pad = pad_all(out_grad)
    active_pad = pad_all(jnp.maximum(pre_act, jnp.zeros((), pre_act.dtype)))
    grad_flat = out_grad.reshape(C, positions)
    act_grad = jnp.zeros((C, positions), jnp.float32)
    filter_two = []
    for offset in range(27):
        act_grad = act_grad + jnp.dot(weight_two[offset], window(grad_pad, offset, True), preferred_element_type=jnp.float32)
        filter_two.append(contract_positions(window(active_pad, offset, False), grad_flat))
    delta = jnp.where(pre_act.reshape(C, positions) > 0, act_grad, 0.0).astype(jnp.bfloat16)
    delta_pad = pad_all(delta.reshape(C, NX, NY, NZ))
    input_grad = jnp.zeros((C, positions), jnp.float32)
    filter_one = []
    for offset in range(27):
        input_grad = input_grad + lax.dot_general(weight_one[offset], window(delta_pad, offset, True), (((0,), (0,)), ((), ())), preferred_element_type=jnp.float32)
        filter_one.append(contract_positions(delta, window(inputs_pad, offset, False)))
    factor = 1.0 / math.sqrt(positions)
    return (input_grad.reshape(C, NX, NY, NZ).astype(jnp.bfloat16), jnp.stack(filter_one) * factor, jnp.stack(filter_two) * factor)
```

```python
import functools

import jax
import jax.numpy as jnp
from jax import lax
from jax.experimental import pallas as pl
from jax.experimental.pallas import tpu as pltpu
from jax.sharding import PartitionSpec as P

BF = jnp.bfloat16
F32 = jnp.float32
LINE = ("sx", "sy")
OFF = 27
OFFP = 28
C = 48
CH = 768
SLAB = 128
NXL = 4
ROWS = OFF * C
ROWSP = OFFP * C
HALF = CH // 2


def place(chip, core):
    return ((chip % 2) * 2 + core) * 2 + chip // 2


SAME_CORE = [[place(chip, core) for chip in range(4)] for core in range(2)]
OTHER_CORE = [(place(x, c), place(x, 1 - c)) for x in range(4) for c in range(2)]


def vmem():
    return pl.BlockSpec(memory_space=pltpu.VMEM)


def smem():
    return pl.BlockSpec(memory_space=pltpu.SMEM)


def call(body, outs, scratch, n_in, limit=48):
    return pl.pallas_call(
        body,
        out_shape=outs,
        in_specs=[smem()] + [vmem()] * n_in,
        out_specs=jax.tree.map(lambda _: vmem(), outs),
        scratch_shapes=scratch,
        compiler_params=pltpu.CompilerParams(vmem_limit_bytes=limit << 20),
    )


def lanes():
    return lax.broadcasted_iota(jnp.int32, (C, SLAB), 1)


def shift_z(part, c, lane):
    if c == 1:
        return part
    z = lane % 64
    if c == 0:
        return jnp.where(z >= 1, pltpu.roll(part, 1, 1), 0.0)
    return jnp.where(z <= 62, pltpu.roll(part, SLAB - 1, 1), 0.0)


def fill_windows(line_ref, stack_ref, sx, sy, mirror, act):
    lane = lanes()
    low = lane < 64
    for xp in range(NXL + 2):
        peer_x = sx + (-1 if xp == 0 else 1 if xp == NXL + 1 else 0)
        valid = jnp.logical_and(peer_x >= 0, peer_x <= 3)
        peer_x = jnp.clip(peer_x, 0, 3)
        at = ((xp - 1) % NXL) * SLAB
        own = line_ref[peer_x * 2 + sy, :, at : at + SLAB].astype(F32)
        oth = line_ref[peer_x * 2 + 1 - sy, :, at : at + SLAB].astype(F32)
        if act:
            own, oth = jnp.maximum(own, 0.0), jnp.maximum(oth, 0.0)
        if xp in (0, NXL + 1):
            own, oth = jnp.where(valid, own, 0.0), jnp.where(valid, oth, 0.0)
        r_own, r_oth = pltpu.roll(own, 64, 1), pltpu.roll(oth, 64, 1)
        rows = (
            jnp.where(low, jnp.where(sy == 1, r_oth, 0.0), r_own),
            own,
            jnp.where(low, r_own, jnp.where(sy == 0, r_oth, 0.0)),
        )
        for b in range(3):
            for c in range(3):
                part = shift_z(rows[b], c, lane).astype(BF)
                for a in range(3):
                    xl = xp - a
                    if 0 <= xl < NXL:
                        o = 9 * a + 3 * b + c
                        o = 26 - o if mirror else o
                        stack_ref[o * C : (o + 1) * C, xl * SLAB : (xl + 1) * SLAB] = part


def nt(left, right):
    return lax.dot_general(left, right, (((1,), (1,)), ((), ())), preferred_element_type=F32)


def act_grad_body(ids, w_ref, g_ref, own_ref, send_ref, u_ref):
    sy = ids[1]
    grad = g_ref[...]
    u_ref[...] = jnp.zeros_like(u_ref)
    for a in range(3):
        for b in range(3):
            o = 9 * a + 3 * b
            y = jnp.dot(w_ref[o * C : (o + 3) * C, :], grad, preferred_element_type=F32)
            u_ref[b, :, a * SLAB : (a + NXL) * SLAB] += y
    lane = lanes()
    low = lane < 64
    for xp in range(NXL + 2):
        at = slice(xp * SLAB, (xp + 1) * SLAB)
        v = [
            sum(shift_z(u_ref[b, c * C : (c + 1) * C, at], 2 - c, lane) for c in range(3))
            for b in range(3)
        ]
        r0, r2 = pltpu.roll(v[0], 64, 1), pltpu.roll(v[2], 64, 1)
        own_ref[:, at] = v[1] + jnp.where(low, r0, r2)
        send_ref[:, at] = jnp.where(
            sy == 0, jnp.where(low, r2, 0.0), jnp.where(low, 0.0, r0)
        )


def filter_body(act, mirror, ids, line_ref, full_ref, keep_ref, send_ref, stack_ref):
    sx, sy, core = ids[0], ids[1], ids[2]
    fill_windows(line_ref, stack_ref, sx, sy, mirror, act)
    mine = full_ref[pl.ds(pl.multiple_of(core * HALF, HALF), HALF), :]
    other = full_ref[pl.ds(pl.multiple_of((1 - core) * HALF, HALF), HALF), :]
    step = 3 * C
    for i in range(9):
        rows = stack_ref[i * step : (i + 1) * step, :]
        send_ref[i * step : (i + 1) * step, :] = nt(rows, other).astype(BF)
        keep_ref[i * step : (i + 1) * step, :] = nt(rows, mine)
    keep_ref[ROWS:ROWSP, :] = jnp.zeros((ROWSP - ROWS, HALF), F32)
    send_ref[ROWS:ROWSP, :] = jnp.zeros((ROWSP - ROWS, HALF), BF)


def data_body(ids, line_ref, w_ref, out_ref, stack_ref):
    fill_windows(line_ref, stack_ref, ids[0], ids[1], True, False)
    for i in range(3):
        out_ref[i * 256 : (i + 1) * 256, :] = jnp.dot(
            w_ref[i * 256 : (i + 1) * 256, :], stack_ref[...], preferred_element_type=F32
        ).astype(BF)


def to_all(x, axis, count, groups=None):
    many = jnp.broadcast_to(x[None], (count,) + x.shape)
    return lax.all_to_all(many, axis, 0, 0, tiled=True, axis_index_groups=groups)


def chip_sum(keep, send):
    got = lax.ppermute(send, LINE, OTHER_CORE)
    return (keep + got.astype(F32)).astype(BF).reshape(4, ROWSP // 4, HALF)


def line_sum(part, factor):
    got = lax.all_to_all(part, LINE, 0, 0, tiled=True, axis_index_groups=SAME_CORE)
    return (got.astype(F32).sum(axis=0) * factor).astype(BF)


def spread(block, core):
    mine = to_all(block, LINE, 4, SAME_CORE).reshape(ROWSP, HALF)[:ROWS]
    other = lax.ppermute(mine, LINE, OTHER_CORE)
    first = jnp.where(core == 0, mine, other)
    second = jnp.where(core == 0, other, mine)
    both = jnp.concatenate([first, second], axis=1).astype(F32)
    return both.reshape(OFF, C, CH)


def shards(inputs, pre_act, out_grad, weight_one, weight_two):
    shape = pre_act.shape
    sx, sy = lax.axis_index("sx"), lax.axis_index("sy")
    core = sx % 2
    ids = jnp.stack([sx, sy, core]).astype(jnp.int32)
    n_pos = NXL * SLAB
    factor = 1.0 / 64.0

    grad = to_all(out_grad.reshape(C, n_pos), "ch", 16).reshape(CH, n_pos)
    pre = pre_act.reshape(C, n_pos)
    pre_line = to_all(pre, LINE, 8)
    full_in = to_all(inputs.reshape(C, n_pos), "ch", 16).reshape(CH, n_pos)
    w_two = weight_two.reshape(ROWS, CH)
    w_one = weight_one.reshape(ROWS, CH).T

    wide = (NXL + 2) * SLAB
    own, over = call(
        act_grad_body,
        (jax.ShapeDtypeStruct((C, wide), F32), jax.ShapeDtypeStruct((C, wide), F32)),
        [pltpu.VMEM((3, 3 * C, wide), F32)],
        2,
    )(ids, w_two, grad)
    own = own + lax.ppermute(over, "sy", [(0, 1), (1, 0)])
    to_left = lax.ppermute(own[:, :SLAB], "sx", [(i + 1, i) for i in range(3)])
    to_right = lax.ppermute(own[:, wide - SLAB :], "sx", [(i, i + 1) for i in range(3)])

    filter_outs = (
        jax.ShapeDtypeStruct((ROWSP, HALF), F32),
        jax.ShapeDtypeStruct((ROWSP, HALF), BF),
    )
    stack = pltpu.VMEM((ROWS, n_pos), BF)
    keep2, send2 = call(functools.partial(filter_body, True, False), filter_outs, [stack], 2)(
        ids, pre_line, grad
    )
    chip2 = chip_sum(keep2, send2)

    mid = own[:, SLAB : wide - SLAB]
    mid = jnp.concatenate(
        [mid[:, :SLAB] + to_right, mid[:, SLAB:-SLAB], mid[:, -SLAB:] + to_left], axis=1
    )
    delta = jnp.where(pre > 0, mid, 0.0).astype(BF)
    delta_line = to_all(delta, LINE, 8)
    block2 = line_sum(chip2, factor)

    keep1, send1 = call(functools.partial(filter_body, False, True), filter_outs, [stack], 2)(
        ids, delta_line, full_in
    )
    chip1 = chip_sum(keep1, send1)
    terms = call(data_body, jax.ShapeDtypeStruct((CH, n_pos), BF), [stack], 2)(
        ids, delta_line, w_one
    )
    filter_two = spread(block2, core)
    block1 = line_sum(chip1, factor)
    got = lax.all_to_all(terms.reshape(16, C, n_pos), "ch", 0, 0, tiled=True)
    input_grad = got.astype(F32).sum(axis=0).astype(BF).reshape(shape)
    filter_one = spread(block1, core)
    return input_grad, filter_one, filter_two


def solution(mesh):
    field = P("ch", "sx", "sy", None)
    filt = P(None, "ch", None)
    return jax.shard_map(
        shards,
        mesh=mesh,
        in_specs=(field, field, field, filt, filt),
        out_specs=(field, filt, filt),
        check_vma=False,
    )
```

```python
import functools

import jax
import jax.numpy as jnp
from jax import lax
from jax.experimental import pallas as pl
from jax.experimental.pallas import tpu as pltpu
from jax.sharding import PartitionSpec as P

BF = jnp.bfloat16
F32 = jnp.float32
LINE = ("sx", "sy")
OFF = 27
OFFP = 28
C = 48
CH = 768
SLAB = 128
NXL = 4
ROWS = OFF * C
ROWSP = OFFP * C
HALF = CH // 2
BLOCK = ROWSP // 4


def place(chip, core):
    return ((chip % 2) * 2 + core) * 2 + chip // 2


OTHER_CORE = [(place(x, c), place(x, 1 - c)) for x in range(4) for c in range(2)]


def vmem():
    return pl.BlockSpec(memory_space=pltpu.VMEM)


def smem():
    return pl.BlockSpec(memory_space=pltpu.SMEM)


def call(body, outs, scratch, n_in, limit=48):
    return pl.pallas_call(
        body,
        out_shape=outs,
        in_specs=[smem()] + [vmem()] * n_in,
        out_specs=jax.tree.map(lambda _: vmem(), outs),
        scratch_shapes=scratch,
        compiler_params=pltpu.CompilerParams(vmem_limit_bytes=limit << 20),
    )


def lanes():
    return lax.broadcasted_iota(jnp.int32, (C, SLAB), 1)


def shift_z(part, c, lane):
    if c == 1:
        return part
    z = lane % 64
    if c == 0:
        return jnp.where(z >= 1, pltpu.roll(part, 1, 1), 0.0)
    return jnp.where(z <= 62, pltpu.roll(part, SLAB - 1, 1), 0.0)


def fill_windows(line_ref, stack_ref, sx, sy, mirror, act):
    lane = lanes()
    low = lane < 64
    for xp in range(NXL + 2):
        peer_x = sx + (-1 if xp == 0 else 1 if xp == NXL + 1 else 0)
        valid = jnp.logical_and(peer_x >= 0, peer_x <= 3)
        peer_x = jnp.clip(peer_x, 0, 3)
        at = ((xp - 1) % NXL) * SLAB
        own = line_ref[peer_x * 2 + sy, :, at : at + SLAB].astype(F32)
        oth = line_ref[peer_x * 2 + 1 - sy, :, at : at + SLAB].astype(F32)
        if act:
            own, oth = jnp.maximum(own, 0.0), jnp.maximum(oth, 0.0)
        if xp in (0, NXL + 1):
            own, oth = jnp.where(valid, own, 0.0), jnp.where(valid, oth, 0.0)
        r_own, r_oth = pltpu.roll(own, 64, 1), pltpu.roll(oth, 64, 1)
        rows = (
            jnp.where(low, jnp.where(sy == 1, r_oth, 0.0), r_own),
            own,
            jnp.where(low, r_own, jnp.where(sy == 0, r_oth, 0.0)),
        )
        for b in range(3):
            for c in range(3):
                part = shift_z(rows[b], c, lane).astype(BF)
                for a in range(3):
                    xl = xp - a
                    if 0 <= xl < NXL:
                        o = 9 * a + 3 * b + c
                        o = 26 - o if mirror else o
                        stack_ref[o * C : (o + 1) * C, xl * SLAB : (xl + 1) * SLAB] = part


def nt(left, right):
    return lax.dot_general(left, right, (((1,), (1,)), ((), ())), preferred_element_type=F32)


def take(both_ref, first, field_ref):
    for k in range(16):
        field_ref[k * C : (k + 1) * C, :] = both_ref[k, first : first + C, :]


def act_grad_body(ids, w_ref, both_ref, own_ref, send_ref, field_ref, u_ref):
    sy = ids[1]
    take(both_ref, 0, field_ref)
    grad = field_ref[...]
    u_ref[...] = jnp.zeros_like(u_ref)
    for a in range(3):
        for b in range(3):
            o = 9 * a + 3 * b
            y = jnp.dot(w_ref[o * C : (o + 3) * C, :], grad, preferred_element_type=F32)
            u_ref[b, :, a * SLAB : (a + NXL) * SLAB] += y
    lane = lanes()
    low = lane < 64
    for xp in range(NXL + 2):
        at = slice(xp * SLAB, (xp + 1) * SLAB)
        v = [
            sum(shift_z(u_ref[b, c * C : (c + 1) * C, at], 2 - c, lane) for c in range(3))
            for b in range(3)
        ]
        r0, r2 = pltpu.roll(v[0], 64, 1), pltpu.roll(v[2], 64, 1)
        own_ref[:, at] = v[1] + jnp.where(low, r0, r2)
        send_ref[:, at] = jnp.where(
            sy == 0, jnp.where(low, r2, 0.0), jnp.where(low, 0.0, r0)
        )


def filter_body(
    act, mirror, first, ids, line_ref, both_ref, keep_ref, send_ref, full_ref, stack_ref
):
    sx, sy, core = ids[0], ids[1], ids[2]
    take(both_ref, first, full_ref)
    fill_windows(line_ref, stack_ref, sx, sy, mirror, act)
    mine = full_ref[pl.ds(pl.multiple_of(core * HALF, HALF), HALF), :]
    other = full_ref[pl.ds(pl.multiple_of((1 - core) * HALF, HALF), HALF), :]
    step = 3 * C
    for i in range(9):
        rows = stack_ref[i * step : (i + 1) * step, :]
        send_ref[i * step : (i + 1) * step, :] = nt(rows, other).astype(BF)
        keep_ref[i * step : (i + 1) * step, :] = nt(rows, mine)
    keep_ref[ROWS:ROWSP, :] = jnp.zeros((ROWSP - ROWS, HALF), F32)
    send_ref[ROWS:ROWSP, :] = jnp.zeros((ROWSP - ROWS, HALF), BF)


def data_body(ids, line_ref, w_ref, out_ref, stack_ref):
    fill_windows(line_ref, stack_ref, ids[0], ids[1], True, False)
    for i in range(3):
        out_ref[i * 256 : (i + 1) * 256, :] = jnp.dot(
            w_ref[i * 256 : (i + 1) * 256, :], stack_ref[...], preferred_element_type=F32
        ).astype(BF)


def to_all(x, axis, count):
    many = jnp.broadcast_to(x[None], (count,) + x.shape)
    return lax.all_to_all(many, axis, 0, 0, tiled=True)


def split_body(ids, keep_ref, got_ref, own_ref, *send_refs):
    chip = ids[3]
    for k in range(4):
        at = pl.ds(pl.multiple_of(((chip + k) % 4) * BLOCK, BLOCK), BLOCK)
        total = keep_ref[at, :] + got_ref[at, :].astype(F32)
        if k == 0:
            own_ref[...] = total
        else:
            send_refs[k - 1][...] = total.astype(BF)


def along(shift):
    return [(place(x, c), place((x + shift) % 4, c)) for x in range(4) for c in range(2)]


def chip_split(ids, keep, got):
    outs = [jax.ShapeDtypeStruct((BLOCK, HALF), F32)]
    outs += [jax.ShapeDtypeStruct((BLOCK, HALF), BF)] * 3
    return call(split_body, tuple(outs), [], 2)(ids, keep, got)


def line_sum(own, one, two, three, factor):
    got = [lax.ppermute(v, LINE, along(k)) for k, v in ((1, one), (3, three), (2, two))]
    total = own
    for v in got:
        total = total + v.astype(F32)
    return (total * factor).astype(BF)


def line_spread(block):
    got = {k: lax.ppermute(block, LINE, along(k)) for k in (1, 3, 2)}
    mine = jnp.concatenate([block, got[1], got[2], got[3]], axis=0)
    return mine, lax.ppermute(mine, LINE, OTHER_CORE)


def write_body(ids, mine_ref, other_ref, out_ref):
    core = ids[2]
    mine = mine_ref[0].astype(F32)
    other = other_ref[0].astype(F32)
    out_ref[:, :, :HALF] = jnp.where(core == 0, mine, other)
    out_ref[:, :, HALF:] = jnp.where(core == 0, other, mine)


def write(ids, mine, other):
    shape = (4, OFFP // 4, C, HALF)
    spec = pl.BlockSpec((1,) + shape[1:], lambda i, ids: ((ids[3] + 4 - i) % 4, 0, 0, 0))
    return pl.pallas_call(
        write_body,
        out_shape=jax.ShapeDtypeStruct((OFF, C, CH), F32),
        grid_spec=pltpu.PrefetchScalarGridSpec(
            num_scalar_prefetch=1,
            grid=(4,),
            in_specs=[spec, spec],
            out_specs=pl.BlockSpec((OFFP // 4, C, CH), lambda i, ids: (i, 0, 0)),
        ),
        compiler_params=pltpu.CompilerParams(vmem_limit_bytes=32 << 20),
    )(ids, mine.reshape(shape), other.reshape(shape))


def shards(inputs, pre_act, out_grad, weight_one, weight_two):
    shape = pre_act.shape
    sx, sy = lax.axis_index("sx"), lax.axis_index("sy")
    core = sx % 2
    chip = sx // 2 + 2 * sy
    ids = jnp.stack([sx, sy, core, chip]).astype(jnp.int32)
    n_pos = NXL * SLAB
    factor = 1.0 / 64.0

    both = jnp.concatenate([out_grad.reshape(C, n_pos), inputs.reshape(C, n_pos)], axis=0)
    both = to_all(both, "ch", 16)
    pre = pre_act.reshape(C, n_pos)
    w_two = weight_two.reshape(ROWS, CH)
    w_one = weight_one.reshape(ROWS, CH).T
    both, w_one, pre = lax.optimization_barrier((both, w_one, pre))
    pre_line = to_all(pre, LINE, 8)

    wide = (NXL + 2) * SLAB
    field = pltpu.VMEM((CH, n_pos), BF)
    own, over = call(
        act_grad_body,
        (jax.ShapeDtypeStruct((C, wide), F32), jax.ShapeDtypeStruct((C, wide), F32)),
        [field, pltpu.VMEM((3, 3 * C, wide), F32)],
        2,
    )(ids, w_two, both)
    own = own + lax.ppermute(over, "sy", [(0, 1), (1, 0)])
    own, pre_line = lax.optimization_barrier((own, pre_line))
    to_left = lax.ppermute(own[:, :SLAB], "sx", [(i + 1, i) for i in range(3)])
    to_right = lax.ppermute(own[:, wide - SLAB :], "sx", [(i, i + 1) for i in range(3)])

    filter_outs = (
        jax.ShapeDtypeStruct((ROWSP, HALF), F32),
        jax.ShapeDtypeStruct((ROWSP, HALF), BF),
    )
    stack = pltpu.VMEM((ROWS, n_pos), BF)
    keep2, send2 = call(
        functools.partial(filter_body, True, False, 0), filter_outs, [field, stack], 2
    )(ids, pre_line, both)
    split2 = chip_split(ids, keep2, lax.ppermute(send2, LINE, OTHER_CORE))

    mid = own[:, SLAB : wide - SLAB]
    mid = jnp.concatenate(
        [mid[:, :SLAB] + to_right, mid[:, SLAB:-SLAB], mid[:, -SLAB:] + to_left], axis=1
    )
    delta = jnp.where(pre > 0, mid, 0.0).astype(BF)
    delta_line = to_all(delta, LINE, 8)
    block2 = line_sum(*split2, factor)

    keep1, send1 = call(
        functools.partial(filter_body, False, True, C), filter_outs, [field, stack], 2
    )(ids, delta_line, both)
    got1 = lax.ppermute(send1, LINE, OTHER_CORE)
    terms = call(data_body, jax.ShapeDtypeStruct((CH, n_pos), BF), [stack], 2)(
        ids, delta_line, w_one
    )
    terms, got1 = lax.optimization_barrier((terms, got1))
    got = lax.all_to_all(terms.reshape(16, C, n_pos), "ch", 0, 0, tiled=True)
    split1 = chip_split(ids, keep1, got1)
    block1 = line_sum(*split1, factor)
    pair2 = line_spread(block2)
    input_grad = got.astype(F32).sum(axis=0).astype(BF).reshape(shape)
    input_grad, block1 = lax.optimization_barrier((input_grad, block1))
    filter_two = write(ids, *pair2)
    filter_one = write(ids, *line_spread(block1))
    return input_grad, filter_one, filter_two


def solution(mesh):
    field = P("ch", "sx", "sy", None)
    filt = P(None, "ch", None)
    return jax.shard_map(
        shards,
        mesh=mesh,
        in_specs=(field, field, field, filt, filt),
        out_specs=(field, filt, filt),
        check_vma=False,
    )
```

```python
import functools

import jax
import jax.numpy as jnp
from jax import lax
from jax.experimental import pallas as pl
from jax.experimental.pallas import tpu as pltpu
from jax.sharding import PartitionSpec as P

BF = jnp.bfloat16
F32 = jnp.float32
LINE = ("sx", "sy")
OFF = 27
OFFP = 28
C = 48
CH = 768
SLAB = 128
NXL = 4
ROWS = OFF * C
ROWSP = OFFP * C
HALF = CH // 2
BLOCK = ROWSP // 4


def place(chip, core):
    return ((chip % 2) * 2 + core) * 2 + chip // 2


OTHER_CORE = [(place(x, c), place(x, 1 - c)) for x in range(4) for c in range(2)]


def vmem():
    return pl.BlockSpec(memory_space=pltpu.VMEM)


def smem():
    return pl.BlockSpec(memory_space=pltpu.SMEM)


def call(body, outs, scratch, n_in, limit=16):
    return pl.pallas_call(
        body,
        out_shape=outs,
        in_specs=[smem()] + [vmem()] * n_in,
        out_specs=jax.tree.map(lambda _: vmem(), outs),
        scratch_shapes=scratch,
        compiler_params=pltpu.CompilerParams(vmem_limit_bytes=limit << 20),
    )


def lanes():
    return lax.broadcasted_iota(jnp.int32, (C, SLAB), 1)


def shift_z(part, c, lane):
    if c == 1:
        return part
    z = lane % 64
    if c == 0:
        return jnp.where(z >= 1, pltpu.roll(part, 1, 1), 0.0)
    return jnp.where(z <= 62, pltpu.roll(part, SLAB - 1, 1), 0.0)


def fill_windows(halo_refs, stack_ref, sy, mirror, act):
    own_ref, left_ref, right_ref, y_ref, y_left_ref, y_right_ref = halo_refs
    lane = lanes()
    low = lane < 64
    for xp in range(NXL + 2):
        at = slice((xp - 1) * SLAB, xp * SLAB)
        if xp == 0:
            own, oth = left_ref[...], y_left_ref[...]
        elif xp == NXL + 1:
            own, oth = right_ref[...], y_right_ref[...]
        else:
            own, oth = own_ref[:, at], y_ref[:, at]
        own, oth = own.astype(F32), oth.astype(F32)
        if act:
            own, oth = jnp.maximum(own, 0.0), jnp.maximum(oth, 0.0)
        r_own, r_oth = pltpu.roll(own, 64, 1), pltpu.roll(oth, 64, 1)
        rows = (
            jnp.where(low, jnp.where(sy == 1, r_oth, 0.0), r_own),
            own,
            jnp.where(low, r_own, jnp.where(sy == 0, r_oth, 0.0)),
        )
        for b in range(3):
            for c in range(3):
                part = shift_z(rows[b], c, lane).astype(BF)
                for a in range(3):
                    xl = xp - a
                    if 0 <= xl < NXL:
                        o = 9 * a + 3 * b + c
                        o = 26 - o if mirror else o
                        stack_ref[o * C : (o + 1) * C, xl * SLAB : (xl + 1) * SLAB] = part


def nt(left, right):
    return lax.dot_general(left, right, (((1,), (1,)), ((), ())), preferred_element_type=F32)


def act_grad_body(
    ids, w_ref, grad_ref, mid_ref, left_ref, right_ref, y_ref, y_left_ref, y_right_ref, u_ref
):
    sy = ids[1]
    grad = grad_ref[...]
    u_ref[...] = jnp.zeros_like(u_ref)
    for a in range(3):
        for b in range(3):
            o = 9 * a + 3 * b
            y = jnp.dot(w_ref[o * C : (o + 3) * C, :], grad, preferred_element_type=F32)
            u_ref[b, :, a * SLAB : (a + NXL) * SLAB] += y
    lane = lanes()
    low = lane < 64
    for xp in range(NXL + 2):
        at = slice(xp * SLAB, (xp + 1) * SLAB)
        v = [
            sum(shift_z(u_ref[b, c * C : (c + 1) * C, at], 2 - c, lane) for c in range(3))
            for b in range(3)
        ]
        r0, r2 = pltpu.roll(v[0], 64, 1), pltpu.roll(v[2], 64, 1)
        own = v[1] + jnp.where(low, r0, r2)
        over = jnp.where(sy == 0, jnp.where(low, r2, 0.0), jnp.where(low, 0.0, r0))
        if xp == 0:
            left_ref[...], y_left_ref[...] = own, over
        elif xp == NXL + 1:
            right_ref[...], y_right_ref[...] = own, over
        else:
            at = slice((xp - 1) * SLAB, xp * SLAB)
            mid_ref[:, at], y_ref[:, at] = own, over


def delta_body(ids, pre_ref, mid_ref, *refs):
    left_ref, right_ref, y_ref, y_left_ref, y_right_ref, out_ref, first_ref, last_ref = refs
    for xl in range(NXL):
        at = slice(xl * SLAB, (xl + 1) * SLAB)
        grad = mid_ref[:, at] + y_ref[:, at]
        if xl == 0:
            grad = grad + left_ref[...] + y_left_ref[...]
        if xl == NXL - 1:
            grad = grad + right_ref[...] + y_right_ref[...]
        delta = jnp.where(pre_ref[:, at].astype(F32) > 0, grad, 0.0).astype(BF)
        out_ref[:, at] = delta
        if xl == 0:
            first_ref[...] = delta
        if xl == NXL - 1:
            last_ref[...] = delta


def filter_body(act, mirror, ids, *refs):
    halo_refs, (full_ref, keep_ref, send_ref, stack_ref) = refs[:6], refs[6:]
    sy, core = ids[1], ids[2]
    fill_windows(halo_refs, stack_ref, sy, mirror, act)
    mine = full_ref[pl.ds(pl.multiple_of(core * HALF, HALF), HALF), :]
    other = full_ref[pl.ds(pl.multiple_of((1 - core) * HALF, HALF), HALF), :]
    step = 3 * C
    for i in range(9):
        rows = stack_ref[i * step : (i + 1) * step, :]
        send_ref[i * step : (i + 1) * step, :] = nt(rows, other).astype(BF)
        keep_ref[i * step : (i + 1) * step, :] = nt(rows, mine)
    keep_ref[ROWS:ROWSP, :] = jnp.zeros((ROWSP - ROWS, HALF), F32)
    send_ref[ROWS:ROWSP, :] = jnp.zeros((ROWSP - ROWS, HALF), BF)


def data_body(ids, *refs):
    halo_refs, (w_ref, out_ref, stack_ref) = refs[:6], refs[6:]
    fill_windows(halo_refs, stack_ref, ids[1], True, False)
    for i in range(3):
        out_ref[i * 256 : (i + 1) * 256, :] = jnp.dot(
            w_ref[i * 256 : (i + 1) * 256, :], stack_ref[...], preferred_element_type=F32
        ).astype(BF)


def to_side(dx, flip):
    return [
        (sx * 2 + sy, (sx + dx) * 2 + (1 - sy if flip else sy))
        for sx in range(4)
        for sy in range(2)
        if 0 <= sx + dx < 4
    ]


def swap(to_left, to_right, whole, y_to_left, y_to_right):
    send = functools.partial(lax.ppermute, axis_name=LINE)
    whole = send(whole, perm=to_side(0, True))
    y_left = send(y_to_right, perm=to_side(1, True))
    y_right = send(y_to_left, perm=to_side(-1, True))
    left = send(to_right, perm=to_side(1, False))
    right = send(to_left, perm=to_side(-1, False))
    return left, right, whole, y_left, y_right


def to_all(x, axis, count):
    many = jnp.broadcast_to(x[None], (count,) + x.shape)
    return lax.all_to_all(many, axis, 0, 0, tiled=True)


def split_body(ids, keep_ref, got_ref, own_ref, *send_refs):
    chip = ids[3]
    for k in range(4):
        at = pl.ds(pl.multiple_of(((chip + k) % 4) * BLOCK, BLOCK), BLOCK)
        total = keep_ref[at, :] + got_ref[at, :].astype(F32)
        if k == 0:
            own_ref[...] = total
        else:
            send_refs[k - 1][...] = total.astype(BF)


def along(shift):
    return [(place(x, c), place((x + shift) % 4, c)) for x in range(4) for c in range(2)]


def chip_split(ids, keep, got):
    outs = [jax.ShapeDtypeStruct((BLOCK, HALF), F32)]
    outs += [jax.ShapeDtypeStruct((BLOCK, HALF), BF)] * 3
    return call(split_body, tuple(outs), [], 2)(ids, keep, got)


def line_sum(own, one, two, three, factor):
    got = [lax.ppermute(v, LINE, along(k)) for k, v in ((1, one), (3, three), (2, two))]
    total = own
    for v in got:
        total = total + v.astype(F32)
    return (total * factor).astype(BF)


def line_spread(block):
    got = {k: lax.ppermute(block, LINE, along(k)) for k in (1, 3, 2)}
    mine = jnp.concatenate([block, got[1], got[2], got[3]], axis=0)
    return mine, lax.ppermute(mine, LINE, OTHER_CORE)


def write_body(ids, mine_ref, other_ref, out_ref):
    core = ids[2]
    mine = mine_ref[0].astype(F32)
    other = other_ref[0].astype(F32)
    out_ref[:, :, :HALF] = jnp.where(core == 0, mine, other)
    out_ref[:, :, HALF:] = jnp.where(core == 0, other, mine)


def write(ids, mine, other):
    shape = (4, OFFP // 4, C, HALF)
    spec = pl.BlockSpec((1,) + shape[1:], lambda i, ids: ((ids[3] + 4 - i) % 4, 0, 0, 0))
    return pl.pallas_call(
        write_body,
        out_shape=jax.ShapeDtypeStruct((OFF, C, CH), F32),
        grid_spec=pltpu.PrefetchScalarGridSpec(
            num_scalar_prefetch=1,
            grid=(4,),
            in_specs=[spec, spec],
            out_specs=pl.BlockSpec((OFFP // 4, C, CH), lambda i, ids: (i, 0, 0)),
        ),
        compiler_params=pltpu.CompilerParams(vmem_limit_bytes=32 << 20),
    )(ids, mine.reshape(shape), other.reshape(shape))


def shards(inputs, pre_act, out_grad, weight_one, weight_two):
    shape = pre_act.shape
    sx, sy = lax.axis_index("sx"), lax.axis_index("sy")
    core = sx % 2
    chip = sx // 2 + 2 * sy
    ids = jnp.stack([sx, sy, core, chip]).astype(jnp.int32)
    n_pos = NXL * SLAB
    factor = 1.0 / 64.0
    edge_f = jax.ShapeDtypeStruct((C, SLAB), F32)
    edge_b = jax.ShapeDtypeStruct((C, SLAB), BF)
    mid_f = jax.ShapeDtypeStruct((C, n_pos), F32)
    mid_b = jax.ShapeDtypeStruct((C, n_pos), BF)

    grad = to_all(out_grad.reshape(C, n_pos), "ch", 16).reshape(CH, n_pos)
    pre = pre_act.reshape(C, n_pos)
    first, last = pre[:, :SLAB], pre[:, n_pos - SLAB :]
    pre_halo = swap(first, last, pre, first, last)
    w_two = weight_two.reshape(ROWS, CH)
    w_one = weight_one.reshape(ROWS, CH).T
    mine_in = inputs.reshape(C, n_pos)
    grad, w_one, mine_in, pre_halo = lax.optimization_barrier((grad, w_one, mine_in, pre_halo))
    full_in = to_all(mine_in, "ch", 16).reshape(CH, n_pos)

    mid, left, right, y_mid, y_left, y_right = call(
        act_grad_body,
        (mid_f, edge_f, edge_f, mid_f, edge_f, edge_f),
        [pltpu.VMEM((3, 3 * C, n_pos + 2 * SLAB), F32)],
        2,
    )(ids, w_two, grad)
    sums = swap(left, right, y_mid, y_left, y_right)

    filter_outs = (
        jax.ShapeDtypeStruct((ROWSP, HALF), F32),
        jax.ShapeDtypeStruct((ROWSP, HALF), BF),
    )
    stack = pltpu.VMEM((ROWS, n_pos), BF)
    keep2, send2 = call(functools.partial(filter_body, True, False), filter_outs, [stack], 7)(
        ids, pre, *pre_halo, grad
    )
    sums, send2 = lax.optimization_barrier((sums, send2))
    got2 = lax.ppermute(send2, LINE, OTHER_CORE)
    delta, first, last = call(delta_body, (mid_b, edge_b, edge_b), [], 7)(ids, pre, mid, *sums)
    halo = swap(first, last, delta, first, last)
    split2 = chip_split(ids, keep2, got2)
    halo, _ = lax.optimization_barrier((halo, split2))

    keep1, send1 = call(functools.partial(filter_body, False, True), filter_outs, [stack], 7)(
        ids, delta, *halo, full_in
    )
    got1 = lax.ppermute(send1, LINE, OTHER_CORE)
    terms = call(data_body, jax.ShapeDtypeStruct((CH, n_pos), BF), [stack], 7)(
        ids, delta, *halo, w_one
    )
    terms, got1 = lax.optimization_barrier((terms, got1))
    got = lax.all_to_all(terms.reshape(16, C, n_pos), "ch", 0, 0, tiled=True)
    block2 = line_sum(*split2, factor)
    split1 = chip_split(ids, keep1, got1)
    block1 = line_sum(*split1, factor)
    pair2 = line_spread(block2)
    input_grad = got.astype(F32).sum(axis=0).astype(BF).reshape(shape)
    input_grad, block1 = lax.optimization_barrier((input_grad, block1))
    filter_two = write(ids, *pair2)
    filter_one = write(ids, *line_spread(block1))
    return input_grad, filter_one, filter_two


def solution(mesh):
    field = P("ch", "sx", "sy", None)
    filt = P(None, "ch", None)
    return jax.shard_map(
        shards,
        mesh=mesh,
        in_specs=(field, field, field, filt, filt),
        out_specs=(field, filt, filt),
        check_vma=False,
    )
```

```python
import functools

import jax
import jax.numpy as jnp
from jax import lax
from jax.experimental import pallas as pl
from jax.experimental.pallas import tpu as pltpu
from jax.sharding import PartitionSpec as P

BF = jnp.bfloat16
F32 = jnp.float32
LINE = ("sx", "sy")
OFF = 27
OFFP = 28
C = 48
CH = 768
SLAB = 128
NXL = 4
ROWS = OFF * C
ROWSP = OFFP * C
HALF = CH // 2
BLOCK = ROWSP // 4


def place(chip, core):
    return ((chip % 2) * 2 + core) * 2 + chip // 2


OTHER_CORE = [(place(x, c), place(x, 1 - c)) for x in range(4) for c in range(2)]


def vmem():
    return pl.BlockSpec(memory_space=pltpu.VMEM)


def smem():
    return pl.BlockSpec(memory_space=pltpu.SMEM)


def call(body, outs, scratch, n_in, limit=16):
    return pl.pallas_call(
        body,
        out_shape=outs,
        in_specs=[smem()] + [vmem()] * n_in,
        out_specs=jax.tree.map(lambda _: vmem(), outs),
        scratch_shapes=scratch,
        compiler_params=pltpu.CompilerParams(vmem_limit_bytes=limit << 20),
    )


def lanes():
    return lax.broadcasted_iota(jnp.int32, (C, SLAB), 1)


def shift_z(part, c, lane):
    if c == 1:
        return part
    z = lane % 64
    if c == 0:
        return jnp.where(z >= 1, pltpu.roll(part, 1, 1), 0.0)
    return jnp.where(z <= 62, pltpu.roll(part, SLAB - 1, 1), 0.0)


def fill_windows(own_ref, oth_ref, stack_ref, sy, mirror, act):
    lane = lanes()
    low = lane < 64
    for xp in range(NXL + 2):
        at = slice(xp * SLAB, (xp + 1) * SLAB)
        own, oth = own_ref[:, at].astype(F32), oth_ref[:, at].astype(F32)
        if act:
            own, oth = jnp.maximum(own, 0.0), jnp.maximum(oth, 0.0)
        r_own, r_oth = pltpu.roll(own, 64, 1), pltpu.roll(oth, 64, 1)
        rows = (
            jnp.where(low, jnp.where(sy == 1, r_oth, 0.0), r_own),
            own,
            jnp.where(low, r_own, jnp.where(sy == 0, r_oth, 0.0)),
        )
        for b in range(3):
            for c in range(3):
                part = shift_z(rows[b], c, lane).astype(BF)
                for a in range(3):
                    xl = xp - a
                    if 0 <= xl < NXL:
                        o = 9 * a + 3 * b + c
                        o = 26 - o if mirror else o
                        stack_ref[o * C : (o + 1) * C, xl * SLAB : (xl + 1) * SLAB] = part


def nt(left, right):
    return lax.dot_general(left, right, (((1,), (1,)), ((), ())), preferred_element_type=F32)


def act_grad_body(ids, w_ref, grad_ref, own_ref, over_ref, pack_ref, u_ref):
    sy = ids[1]
    grad = grad_ref[...]
    u_ref[...] = jnp.zeros_like(u_ref)
    for a in range(3):
        for b in range(3):
            o = 9 * a + 3 * b
            y = jnp.dot(w_ref[o * C : (o + 3) * C, :], grad, preferred_element_type=F32)
            u_ref[b, :, a * SLAB : (a + NXL) * SLAB] += y
    lane = lanes()
    low = lane < 64
    for xp in range(NXL + 2):
        at = slice(xp * SLAB, (xp + 1) * SLAB)
        v = [
            sum(shift_z(u_ref[b, c * C : (c + 1) * C, at], 2 - c, lane) for c in range(3))
            for b in range(3)
        ]
        r0, r2 = pltpu.roll(v[0], 64, 1), pltpu.roll(v[2], 64, 1)
        own = v[1] + jnp.where(low, r0, r2)
        over = jnp.where(sy == 0, jnp.where(low, r2, 0.0), jnp.where(low, 0.0, r0))
        own_ref[:, at], over_ref[:, at] = own, over
        pack_ref[:, at] = jnp.where(low, jnp.where(sy == 0, over, own), jnp.where(sy == 0, own, over))


def join_y_body(ids, own_ref, over_ref, pack_ref, own_out, oth_out, left_out, right_out):
    sy = ids[1]
    low = lanes() < 64
    for xp in range(NXL + 2):
        at = slice(xp * SLAB, (xp + 1) * SLAB)
        pack = pack_ref[:, at]
        lower, upper = jnp.where(low, pack, 0.0), jnp.where(low, 0.0, pack)
        own = own_ref[:, at] + jnp.where(sy == 0, upper, lower)
        oth = over_ref[:, at] + jnp.where(sy == 0, lower, upper)
        own_out[:, at], oth_out[:, at] = own, oth
        for out, first in ((left_out, 0), (right_out, NXL)):
            if first <= xp < first + 2:
                k = (xp - first) * SLAB
                out[:, k : k + SLAB] = own
                out[:, k + 2 * SLAB : k + 3 * SLAB] = oth


def delta_body(ids, own_ref, oth_ref, left_ref, right_ref, pre_own_ref, pre_oth_ref, own_out, oth_out):
    for xp in range(NXL + 2):
        at = slice(xp * SLAB, (xp + 1) * SLAB)
        for grad_ref, pre_ref, out, half in (
            (own_ref, pre_own_ref, own_out, 0),
            (oth_ref, pre_oth_ref, oth_out, 2 * SLAB),
        ):
            grad = grad_ref[:, at]
            if xp < 2:
                k = half + xp * SLAB
                grad = grad + left_ref[:, k : k + SLAB]
            if xp >= NXL:
                k = half + (xp - NXL) * SLAB
                grad = grad + right_ref[:, k : k + SLAB]
            out[:, at] = jnp.where(pre_ref[:, at].astype(F32) > 0, grad, 0.0).astype(BF)


def filter_body(act, mirror, ids, *refs):
    own_ref, oth_ref, full_ref, keep_ref, send_ref, stack_ref = refs
    sy, core = ids[1], ids[2]
    fill_windows(own_ref, oth_ref, stack_ref, sy, mirror, act)
    mine = full_ref[pl.ds(pl.multiple_of(core * HALF, HALF), HALF), :]
    other = full_ref[pl.ds(pl.multiple_of((1 - core) * HALF, HALF), HALF), :]
    step = 3 * C
    for i in range(9):
        rows = stack_ref[i * step : (i + 1) * step, :]
        send_ref[i * step : (i + 1) * step, :] = nt(rows, other).astype(BF)
        keep_ref[i * step : (i + 1) * step, :] = nt(rows, mine)
    keep_ref[ROWS:ROWSP, :] = jnp.zeros((ROWSP - ROWS, HALF), F32)
    send_ref[ROWS:ROWSP, :] = jnp.zeros((ROWSP - ROWS, HALF), BF)


def data_body(ids, *refs):
    own_ref, oth_ref, w_ref, out_ref, stack_ref = refs
    fill_windows(own_ref, oth_ref, stack_ref, ids[1], True, False)
    for i in range(3):
        out_ref[i * 256 : (i + 1) * 256, :] = jnp.dot(
            w_ref[i * 256 : (i + 1) * 256, :], stack_ref[...], preferred_element_type=F32
        ).astype(BF)


def to_side(dx, flip):
    return [
        (sx * 2 + sy, (sx + dx) * 2 + (1 - sy if flip else sy))
        for sx in range(4)
        for sy in range(2)
        if 0 <= sx + dx < 4
    ]


def halo(whole):
    send = functools.partial(lax.ppermute, axis_name=LINE)
    first, last = whole[:, :SLAB], whole[:, whole.shape[1] - SLAB :]
    sides = []
    for flip, mid in ((False, whole), (True, send(whole, perm=to_side(0, True)))):
        left = send(last, perm=to_side(1, flip))
        right = send(first, perm=to_side(-1, flip))
        sides.append(jnp.concatenate([left, mid, right], axis=1))
    return tuple(sides)


def to_all(x, axis, count):
    many = jnp.broadcast_to(x[None], (count,) + x.shape)
    return lax.all_to_all(many, axis, 0, 0, tiled=True)


def split_body(ids, keep_ref, got_ref, own_ref, *send_refs):
    chip = ids[3]
    for k in range(4):
        at = pl.ds(pl.multiple_of(((chip + k) % 4) * BLOCK, BLOCK), BLOCK)
        total = keep_ref[at, :] + got_ref[at, :].astype(F32)
        if k == 0:
            own_ref[...] = total
        else:
            send_refs[k - 1][...] = total.astype(BF)


def along(shift):
    return [(place(x, c), place((x + shift) % 4, c)) for x in range(4) for c in range(2)]


def chip_split(ids, keep, got):
    outs = [jax.ShapeDtypeStruct((BLOCK, HALF), F32)]
    outs += [jax.ShapeDtypeStruct((BLOCK, HALF), BF)] * 3
    return call(split_body, tuple(outs), [], 2)(ids, keep, got)


def line_sum(own, one, two, three, factor):
    got = [lax.ppermute(v, LINE, along(k)) for k, v in ((1, one), (3, three), (2, two))]
    total = own
    for v in got:
        total = total + v.astype(F32)
    return (total * factor).astype(BF)


def line_spread(block):
    got = {k: lax.ppermute(block, LINE, along(k)) for k in (1, 3, 2)}
    mine = jnp.concatenate([block, got[1], got[2], got[3]], axis=0)
    return mine, lax.ppermute(mine, LINE, OTHER_CORE)


def write_body(ids, mine_ref, other_ref, out_ref):
    core = ids[2]
    mine = mine_ref[0].astype(F32)
    other = other_ref[0].astype(F32)
    out_ref[:, :, :HALF] = jnp.where(core == 0, mine, other)
    out_ref[:, :, HALF:] = jnp.where(core == 0, other, mine)


def write(ids, mine, other):
    shape = (4, OFFP // 4, C, HALF)
    spec = pl.BlockSpec((1,) + shape[1:], lambda i, ids: ((ids[3] + 4 - i) % 4, 0, 0, 0))
    return pl.pallas_call(
        write_body,
        out_shape=jax.ShapeDtypeStruct((OFF, C, CH), F32),
        grid_spec=pltpu.PrefetchScalarGridSpec(
            num_scalar_prefetch=1,
            grid=(4,),
            in_specs=[spec, spec],
            out_specs=pl.BlockSpec((OFFP // 4, C, CH), lambda i, ids: (i, 0, 0)),
        ),
        compiler_params=pltpu.CompilerParams(vmem_limit_bytes=32 << 20),
    )(ids, mine.reshape(shape), other.reshape(shape))


def shards(inputs, pre_act, out_grad, weight_one, weight_two):
    shape = pre_act.shape
    sx, sy = lax.axis_index("sx"), lax.axis_index("sy")
    core = sx % 2
    chip = sx // 2 + 2 * sy
    ids = jnp.stack([sx, sy, core, chip]).astype(jnp.int32)
    n_pos = NXL * SLAB
    factor = 1.0 / 64.0
    wide = n_pos + 2 * SLAB
    wide_f = jax.ShapeDtypeStruct((C, wide), F32)
    wide_b = jax.ShapeDtypeStruct((C, wide), BF)
    mid_f = jax.ShapeDtypeStruct((C, n_pos), F32)

    grad = to_all(out_grad.reshape(C, n_pos), "ch", 16).reshape(CH, n_pos)
    pre = halo(pre_act.reshape(C, n_pos))
    w_two = weight_two.reshape(ROWS, CH)
    w_one = weight_one.reshape(ROWS, CH).T
    mine_in = inputs.reshape(C, n_pos)
    grad, w_one, mine_in, pre = lax.optimization_barrier((grad, w_one, mine_in, pre))
    full_in = to_all(mine_in, "ch", 16).reshape(CH, n_pos)

    own, over, pack = call(
        act_grad_body,
        (wide_f, wide_f, wide_f),
        [pltpu.VMEM((3, 3 * C, wide), F32)],
        2,
    )(ids, w_two, grad)
    pack = lax.ppermute(pack, LINE, to_side(0, True))

    filter_outs = (
        jax.ShapeDtypeStruct((ROWSP, HALF), F32),
        jax.ShapeDtypeStruct((ROWSP, HALF), BF),
    )
    stack = pltpu.VMEM((ROWS, n_pos), BF)
    keep2, send2 = call(functools.partial(filter_body, True, False), filter_outs, [stack], 3)(
        ids, *pre, grad
    )
    pack, send2 = lax.optimization_barrier((pack, send2))
    own, oth, left, right = call(join_y_body, (wide_f, wide_f, mid_f, mid_f), [], 3)(
        ids, own, over, pack
    )
    from_left = lax.ppermute(right, LINE, to_side(1, False))
    from_right = lax.ppermute(left, LINE, to_side(-1, False))
    got2 = lax.ppermute(send2, LINE, OTHER_CORE)
    split2 = chip_split(ids, keep2, got2)
    from_left, from_right, full_in, _ = lax.optimization_barrier(
        (from_left, from_right, full_in, split2)
    )
    delta = call(delta_body, (wide_b, wide_b), [], 6)(
        ids, own, oth, from_left, from_right, *pre
    )

    keep1, send1 = call(functools.partial(filter_body, False, True), filter_outs, [stack], 3)(
        ids, *delta, full_in
    )
    got1 = lax.ppermute(send1, LINE, OTHER_CORE)
    split1 = chip_split(ids, keep1, got1)
    delta, _ = lax.optimization_barrier((delta, split1))
    terms = call(data_body, jax.ShapeDtypeStruct((CH, n_pos), BF), [stack], 3)(
        ids, *delta, w_one
    )
    got = lax.all_to_all(terms.reshape(16, C, n_pos), "ch", 0, 0, tiled=True)
    block2 = line_sum(*split2, factor)
    block1 = line_sum(*split1, factor)
    pair2 = line_spread(block2)
    input_grad = got.astype(F32).sum(axis=0).astype(BF).reshape(shape)
    input_grad, block1 = lax.optimization_barrier((input_grad, block1))
    filter_two = write(ids, *pair2)
    filter_one = write(ids, *line_spread(block1))
    return input_grad, filter_one, filter_two


def solution(mesh):
    field = P("ch", "sx", "sy", None)
    filt = P(None, "ch", None)
    return jax.shard_map(
        shards,
        mesh=mesh,
        in_specs=(field, field, field, filt, filt),
        out_specs=(field, filt, filt),
        check_vma=False,
    )
```

```python
import functools

import jax
import jax.numpy as jnp
from jax import lax
from jax.experimental import pallas as pl
from jax.experimental.pallas import tpu as pltpu
from jax.sharding import PartitionSpec as P

BF = jnp.bfloat16
F32 = jnp.float32
LINE = ("sx", "sy")
OFF = 27
OFFP = 28
C = 48
CH = 768
SLAB = 128
NXL = 4
ROWS = OFF * C
ROWSP = OFFP * C
HALF = CH // 2
BLOCK = ROWSP // 4


def place(chip, core):
    return ((chip % 2) * 2 + core) * 2 + chip // 2


OTHER_CORE = [(place(x, c), place(x, 1 - c)) for x in range(4) for c in range(2)]


def vmem():
    return pl.BlockSpec(memory_space=pltpu.VMEM)


def smem():
    return pl.BlockSpec(memory_space=pltpu.SMEM)


def call(body, outs, scratch, n_in, limit=16):
    return pl.pallas_call(
        body,
        out_shape=outs,
        in_specs=[smem()] + [vmem()] * n_in,
        out_specs=jax.tree.map(lambda _: vmem(), outs),
        scratch_shapes=scratch,
        compiler_params=pltpu.CompilerParams(vmem_limit_bytes=limit << 20),
    )


def lanes():
    return lax.broadcasted_iota(jnp.int32, (C, SLAB), 1)


def shift_z(part, c, lane):
    if c == 1:
        return part
    z = lane % 64
    if c == 0:
        return jnp.where(z >= 1, pltpu.roll(part, 1, 1), 0.0)
    return jnp.where(z <= 62, pltpu.roll(part, SLAB - 1, 1), 0.0)


def fill_windows(own_ref, oth_ref, stack_ref, sy, mirror, act):
    lane = lanes()
    low = lane < 64
    for xp in range(NXL + 2):
        at = slice(xp * SLAB, (xp + 1) * SLAB)
        own, oth = own_ref[:, at].astype(F32), oth_ref[:, at].astype(F32)
        if act:
            own, oth = jnp.maximum(own, 0.0), jnp.maximum(oth, 0.0)
        r_own, r_oth = pltpu.roll(own, 64, 1), pltpu.roll(oth, 64, 1)
        rows = (
            jnp.where(low, jnp.where(sy == 1, r_oth, 0.0), r_own),
            own,
            jnp.where(low, r_own, jnp.where(sy == 0, r_oth, 0.0)),
        )
        for b in range(3):
            for c in range(3):
                part = shift_z(rows[b], c, lane).astype(BF)
                for a in range(3):
                    xl = xp - a
                    if 0 <= xl < NXL:
                        o = 9 * a + 3 * b + c
                        o = 26 - o if mirror else o
                        stack_ref[o * C : (o + 1) * C, xl * SLAB : (xl + 1) * SLAB] = part


def nt(left, right):
    return lax.dot_general(left, right, (((1,), (1,)), ((), ())), preferred_element_type=F32)


def act_grad_body(ids, w_ref, grad_ref, own_ref, over_ref, pack_ref, u_ref):
    sy = ids[1]
    grad = grad_ref[...]
    u_ref[...] = jnp.zeros_like(u_ref)
    for a in range(3):
        for b in range(3):
            o = 9 * a + 3 * b
            y = jnp.dot(w_ref[o * C : (o + 3) * C, :], grad, preferred_element_type=F32)
            u_ref[b, :, a * SLAB : (a + NXL) * SLAB] += y
    lane = lanes()
    low = lane < 64
    for xp in range(NXL + 2):
        at = slice(xp * SLAB, (xp + 1) * SLAB)
        v = [
            sum(shift_z(u_ref[b, c * C : (c + 1) * C, at], 2 - c, lane) for c in range(3))
            for b in range(3)
        ]
        r0, r2 = pltpu.roll(v[0], 64, 1), pltpu.roll(v[2], 64, 1)
        own = v[1] + jnp.where(low, r0, r2)
        over = jnp.where(sy == 0, jnp.where(low, r2, 0.0), jnp.where(low, 0.0, r0))
        own_ref[:, at], over_ref[:, at] = own, over
        pack_ref[:, at] = jnp.where(low, jnp.where(sy == 0, over, own), jnp.where(sy == 0, own, over))


def join_y_body(ids, own_ref, over_ref, pack_ref, own_out, oth_out, left_out, right_out):
    sy = ids[1]
    low = lanes() < 64
    for xp in range(NXL + 2):
        at = slice(xp * SLAB, (xp + 1) * SLAB)
        pack = pack_ref[:, at]
        lower, upper = jnp.where(low, pack, 0.0), jnp.where(low, 0.0, pack)
        own = own_ref[:, at] + jnp.where(sy == 0, upper, lower)
        oth = over_ref[:, at] + jnp.where(sy == 0, lower, upper)
        own_out[:, at], oth_out[:, at] = own, oth
        for out, first in ((left_out, 0), (right_out, NXL)):
            if first <= xp < first + 2:
                k = (xp - first) * SLAB
                out[:, k : k + SLAB] = own
                out[:, k + 2 * SLAB : k + 3 * SLAB] = oth


def delta_body(ids, own_ref, oth_ref, left_ref, right_ref, pre_own_ref, pre_oth_ref, own_out, oth_out):
    for xp in range(NXL + 2):
        at = slice(xp * SLAB, (xp + 1) * SLAB)
        for grad_ref, pre_ref, out, half in (
            (own_ref, pre_own_ref, own_out, 0),
            (oth_ref, pre_oth_ref, oth_out, 2 * SLAB),
        ):
            grad = grad_ref[:, at]
            if xp < 2:
                k = half + xp * SLAB
                grad = grad + left_ref[:, k : k + SLAB]
            if xp >= NXL:
                k = half + (xp - NXL) * SLAB
                grad = grad + right_ref[:, k : k + SLAB]
            out[:, at] = jnp.where(pre_ref[:, at].astype(F32) > 0, grad, 0.0).astype(BF)


def send_body(act, mirror, ids, own_ref, oth_ref, full_ref, send_ref, stack_ref):
    sy, core = ids[1], ids[2]
    fill_windows(own_ref, oth_ref, stack_ref, sy, mirror, act)
    other = full_ref[pl.ds(pl.multiple_of((1 - core) * HALF, HALF), HALF), :]
    for i in range(9):
        at = slice(i * 3 * C, (i + 1) * 3 * C)
        send_ref[at, :] = nt(stack_ref[at, :], other).astype(BF)
    send_ref[ROWS:ROWSP, :] = jnp.zeros((ROWSP - ROWS, HALF), BF)


def keep_body(act, mirror, ids, own_ref, oth_ref, full_ref, got_ref, keep_ref, *refs):
    send_refs, stack_ref = refs[:3], refs[3]
    sy, core, chip = ids[1], ids[2], ids[3]
    fill_windows(own_ref, oth_ref, stack_ref, sy, mirror, act)
    stack_ref[ROWS:ROWSP, :] = jnp.zeros((ROWSP - ROWS, NXL * SLAB), BF)
    mine = full_ref[pl.ds(pl.multiple_of(core * HALF, HALF), HALF), :]
    for k in (1, 3, 2, 0):
        for part in range(2):
            n = BLOCK // 2 - 8 * (1 - 2 * part)
            first = part * 160
            at = pl.ds(pl.multiple_of(((chip + k) % 4) * BLOCK + first, 16), n)
            total = nt(stack_ref[at, :], mine) + got_ref[at, :].astype(F32)
            to = slice(first, first + n)
            if k == 0:
                keep_ref[to, :] = total
            else:
                send_refs[k - 1][to, :] = total.astype(BF)


def data_body(ids, *refs):
    own_ref, oth_ref, w_ref, out_ref, stack_ref = refs
    fill_windows(own_ref, oth_ref, stack_ref, ids[1], True, False)
    for i in range(3):
        out_ref[i * 256 : (i + 1) * 256, :] = jnp.dot(
            w_ref[i * 256 : (i + 1) * 256, :], stack_ref[...], preferred_element_type=F32
        ).astype(BF)


def to_side(dx, flip):
    return [
        (sx * 2 + sy, (sx + dx) * 2 + (1 - sy if flip else sy))
        for sx in range(4)
        for sy in range(2)
        if 0 <= sx + dx < 4
    ]


def halo(whole):
    send = functools.partial(lax.ppermute, axis_name=LINE)
    first, last = whole[:, :SLAB], whole[:, whole.shape[1] - SLAB :]
    sides = []
    for flip, mid in ((False, whole), (True, send(whole, perm=to_side(0, True)))):
        left = send(last, perm=to_side(1, flip))
        right = send(first, perm=to_side(-1, flip))
        sides.append(jnp.concatenate([left, mid, right], axis=1))
    return tuple(sides)


def to_all(x, axis, count):
    many = jnp.broadcast_to(x[None], (count,) + x.shape)
    return lax.all_to_all(many, axis, 0, 0, tiled=True)


def along(shift):
    return [(place(x, c), place((x + shift) % 4, c)) for x in range(4) for c in range(2)]


def filter_sums(ids, own, oth, full, act, mirror):
    n_pos = NXL * SLAB
    sent = jax.ShapeDtypeStruct((ROWSP, HALF), BF)
    outs = [jax.ShapeDtypeStruct((BLOCK, HALF), F32)]
    outs += [jax.ShapeDtypeStruct((BLOCK, HALF), BF)] * 3

    def send():
        stack = pltpu.VMEM((ROWS, n_pos), BF)
        body = functools.partial(send_body, act, mirror)
        return call(body, sent, [stack], 3)(ids, own, oth, full)

    def keep(got):
        stack = pltpu.VMEM((ROWSP, n_pos), BF)
        body = functools.partial(keep_body, act, mirror)
        return call(body, tuple(outs), [stack], 4)(ids, own, oth, full, got)

    return send, keep


def arrive(split):
    own, one, two, three = split
    return [own] + [lax.ppermute(v, LINE, along(k)) for k, v in ((1, one), (3, three), (2, two))]


def line_sum(parts, factor, after=None):
    if after is not None:
        parts, _ = lax.optimization_barrier((parts, after))
    total = parts[0]
    for v in parts[1:]:
        total = total + v.astype(F32)
    return (total * factor).astype(BF)


def line_spread(block, after=None):
    got = {k: lax.ppermute(block, LINE, along(k)) for k in (1, 3, 2)}
    if after is not None:
        got, _ = lax.optimization_barrier((got, after))
    mine = jnp.concatenate([block, got[1], got[2], got[3]], axis=0)
    return mine, lax.ppermute(mine, LINE, OTHER_CORE)


def write_body(ids, mine_ref, other_ref, out_ref):
    core = ids[2]
    mine = mine_ref[0].astype(F32)
    other = other_ref[0].astype(F32)
    out_ref[:, :, :HALF] = jnp.where(core == 0, mine, other)
    out_ref[:, :, HALF:] = jnp.where(core == 0, other, mine)


def write(ids, mine, other):
    shape = (4, OFFP // 4, C, HALF)
    spec = pl.BlockSpec((1,) + shape[1:], lambda i, ids: ((ids[3] + 4 - i) % 4, 0, 0, 0))
    return pl.pallas_call(
        write_body,
        out_shape=jax.ShapeDtypeStruct((OFF, C, CH), F32),
        grid_spec=pltpu.PrefetchScalarGridSpec(
            num_scalar_prefetch=1,
            grid=(4,),
            in_specs=[spec, spec],
            out_specs=pl.BlockSpec((OFFP // 4, C, CH), lambda i, ids: (i, 0, 0)),
        ),
        compiler_params=pltpu.CompilerParams(vmem_limit_bytes=32 << 20),
    )(ids, mine.reshape(shape), other.reshape(shape))


def shards(inputs, pre_act, out_grad, weight_one, weight_two):
    shape = pre_act.shape
    sx, sy = lax.axis_index("sx"), lax.axis_index("sy")
    core = sx % 2
    chip = sx // 2 + 2 * sy
    ids = jnp.stack([sx, sy, core, chip]).astype(jnp.int32)
    n_pos = NXL * SLAB
    factor = 1.0 / 64.0
    wide = n_pos + 2 * SLAB
    wide_f = jax.ShapeDtypeStruct((C, wide), F32)
    wide_b = jax.ShapeDtypeStruct((C, wide), BF)
    mid_f = jax.ShapeDtypeStruct((C, n_pos), F32)

    grad = to_all(out_grad.reshape(C, n_pos), "ch", 16).reshape(CH, n_pos)
    pre = halo(pre_act.reshape(C, n_pos))
    w_two = weight_two.reshape(ROWS, CH)
    w_one = weight_one.reshape(ROWS, CH).T
    mine_in = inputs.reshape(C, n_pos)
    many_in = jnp.broadcast_to(mine_in[None], (16, C, n_pos))
    grad, w_one, many_in, pre = lax.optimization_barrier((grad, w_one, many_in, pre))
    full_in = lax.all_to_all(many_in, "ch", 0, 0, tiled=True).reshape(CH, n_pos)

    own, over, pack = call(
        act_grad_body,
        (wide_f, wide_f, wide_f),
        [pltpu.VMEM((3, 3 * C, wide), F32)],
        2,
    )(ids, w_two, grad)
    pack = lax.ppermute(pack, LINE, to_side(0, True))

    send_two, keep_two = filter_sums(ids, *pre, grad, True, False)
    send2 = send_two()
    pack, send2, full_in = lax.optimization_barrier((pack, send2, full_in))
    got2 = lax.ppermute(send2, LINE, OTHER_CORE)
    own, oth, left, right = call(join_y_body, (wide_f, wide_f, mid_f, mid_f), [], 3)(
        ids, own, over, pack
    )
    from_left = lax.ppermute(right, LINE, to_side(1, False))
    from_right = lax.ppermute(left, LINE, to_side(-1, False))
    split2 = keep_two(got2)
    from_left, from_right, _ = lax.optimization_barrier((from_left, from_right, split2))
    delta = call(delta_body, (wide_b, wide_b), [], 6)(
        ids, own, oth, from_left, from_right, *pre
    )

    arrive2 = arrive(split2)
    send_one, keep_one = filter_sums(ids, *delta, full_in, False, True)
    got1 = lax.ppermute(send_one(), LINE, OTHER_CORE)
    split1 = keep_one(got1)
    delta, _ = lax.optimization_barrier((delta, split1))
    terms = call(
        data_body,
        jax.ShapeDtypeStruct((CH, n_pos), BF),
        [pltpu.VMEM((ROWS, n_pos), BF)],
        3,
    )(ids, *delta, w_one)
    got = lax.all_to_all(terms.reshape(16, C, n_pos), "ch", 0, 0, tiled=True)
    block2 = line_sum(arrive2, factor)
    block1 = line_sum(arrive(split1), factor, terms)
    filter_two = write(ids, *line_spread(block2, (block1, got)))
    input_grad = got.astype(F32).sum(axis=0).astype(BF).reshape(shape)
    filter_one = write(ids, *line_spread(block1, (filter_two, input_grad)))
    return input_grad, filter_one, filter_two


def solution(mesh):
    field = P("ch", "sx", "sy", None)
    filt = P(None, "ch", None)
    return jax.shard_map(
        shards,
        mesh=mesh,
        in_specs=(field, field, field, filt, filt),
        out_specs=(field, filt, filt),
        check_vma=False,
    )
```

```python
import functools

import jax
import jax.numpy as jnp
from jax import lax
from jax.experimental import pallas as pl
from jax.experimental.pallas import tpu as pltpu
from jax.sharding import PartitionSpec as P

BF = jnp.bfloat16
F32 = jnp.float32
LINE = ("sx", "sy")
OFF = 27
OFFP = 28
C = 48
CH = 768
SLAB = 128
NXL = 4
ROWS = OFF * C
ROWSP = OFFP * C
HALF = CH // 2
BLOCK = ROWSP // 4


def place(chip, core):
    return ((chip % 2) * 2 + core) * 2 + chip // 2


OTHER_CORE = [(place(x, c), place(x, 1 - c)) for x in range(4) for c in range(2)]


def vmem():
    return pl.BlockSpec(memory_space=pltpu.VMEM)


def smem():
    return pl.BlockSpec(memory_space=pltpu.SMEM)


def call(body, outs, scratch, n_in, limit=16):
    return pl.pallas_call(
        body,
        out_shape=outs,
        in_specs=[smem()] + [vmem()] * n_in,
        out_specs=jax.tree.map(lambda _: vmem(), outs),
        scratch_shapes=scratch,
        compiler_params=pltpu.CompilerParams(vmem_limit_bytes=limit << 20),
    )


def lanes():
    return lax.broadcasted_iota(jnp.int32, (C, SLAB), 1)


def shift_z(part, c, lane):
    if c == 1:
        return part
    z = lane % 64
    if c == 0:
        return jnp.where(z >= 1, pltpu.roll(part, 1, 1), 0.0)
    return jnp.where(z <= 62, pltpu.roll(part, SLAB - 1, 1), 0.0)


def fill_windows(own_ref, oth_ref, stack_ref, sy, mirror, act):
    lane = lanes()
    low = lane < 64
    for xp in range(NXL + 2):
        at = slice(xp * SLAB, (xp + 1) * SLAB)
        own, oth = own_ref[:, at].astype(F32), oth_ref[:, at].astype(F32)
        if act:
            own, oth = jnp.maximum(own, 0.0), jnp.maximum(oth, 0.0)
        r_own, r_oth = pltpu.roll(own, 64, 1), pltpu.roll(oth, 64, 1)
        rows = (
            jnp.where(low, jnp.where(sy == 1, r_oth, 0.0), r_own),
            own,
            jnp.where(low, r_own, jnp.where(sy == 0, r_oth, 0.0)),
        )
        for b in range(3):
            for c in range(3):
                part = shift_z(rows[b], c, lane).astype(BF)
                for a in range(3):
                    xl = xp - a
                    if 0 <= xl < NXL:
                        o = 9 * a + 3 * b + c
                        o = 26 - o if mirror else o
                        stack_ref[o * C : (o + 1) * C, xl * SLAB : (xl + 1) * SLAB] = part


def nt(left, right):
    return lax.dot_general(left, right, (((1,), (1,)), ((), ())), preferred_element_type=F32)


def take(both_ref, second, field_ref):
    for k in range(16):
        field_ref[k * C : (k + 1) * C, :] = both_ref[k, second * C : (second + 1) * C, :]


def act_grad_body(ids, w_ref, both_ref, own_ref, over_ref, pack_ref, field_ref, u_ref):
    sy = ids[1]
    take(both_ref, 0, field_ref)
    grad = field_ref[...]
    u_ref[...] = jnp.zeros_like(u_ref)
    for a in range(3):
        for b in range(3):
            o = 9 * a + 3 * b
            y = jnp.dot(w_ref[o * C : (o + 3) * C, :], grad, preferred_element_type=F32)
            u_ref[b, :, a * SLAB : (a + NXL) * SLAB] += y
    lane = lanes()
    low = lane < 64
    for xp in range(NXL + 2):
        at = slice(xp * SLAB, (xp + 1) * SLAB)
        v = [
            sum(shift_z(u_ref[b, c * C : (c + 1) * C, at], 2 - c, lane) for c in range(3))
            for b in range(3)
        ]
        r0, r2 = pltpu.roll(v[0], 64, 1), pltpu.roll(v[2], 64, 1)
        own = v[1] + jnp.where(low, r0, r2)
        over = jnp.where(sy == 0, jnp.where(low, r2, 0.0), jnp.where(low, 0.0, r0))
        own_ref[:, at], over_ref[:, at] = own, over
        pack_ref[:, at] = jnp.where(low, jnp.where(sy == 0, over, own), jnp.where(sy == 0, own, over))


def join_y_body(ids, own_ref, over_ref, pack_ref, own_out, oth_out, left_out, right_out):
    sy = ids[1]
    low = lanes() < 64
    for xp in range(NXL + 2):
        at = slice(xp * SLAB, (xp + 1) * SLAB)
        pack = pack_ref[:, at]
        lower, upper = jnp.where(low, pack, 0.0), jnp.where(low, 0.0, pack)
        own = own_ref[:, at] + jnp.where(sy == 0, upper, lower)
        oth = over_ref[:, at] + jnp.where(sy == 0, lower, upper)
        own_out[:, at], oth_out[:, at] = own, oth
        for out, first in ((left_out, 0), (right_out, NXL)):
            if first <= xp < first + 2:
                k = (xp - first) * SLAB
                out[:, k : k + SLAB] = own
                out[:, k + 2 * SLAB : k + 3 * SLAB] = oth


def delta_body(ids, own_ref, oth_ref, left_ref, right_ref, pre_own_ref, pre_oth_ref, own_out, oth_out):
    for xp in range(NXL + 2):
        at = slice(xp * SLAB, (xp + 1) * SLAB)
        for grad_ref, pre_ref, out, half in (
            (own_ref, pre_own_ref, own_out, 0),
            (oth_ref, pre_oth_ref, oth_out, 2 * SLAB),
        ):
            grad = grad_ref[:, at]
            if xp < 2:
                k = half + xp * SLAB
                grad = grad + left_ref[:, k : k + SLAB]
            if xp >= NXL:
                k = half + (xp - NXL) * SLAB
                grad = grad + right_ref[:, k : k + SLAB]
            out[:, at] = jnp.where(pre_ref[:, at].astype(F32) > 0, grad, 0.0).astype(BF)


def send_body(act, ids, own_ref, oth_ref, both_ref, send_ref, stack_ref, full_ref):
    sy, core = ids[1], ids[2]
    take(both_ref, 0 if act else 1, full_ref)
    fill_windows(own_ref, oth_ref, stack_ref, sy, not act, act)
    other = full_ref[pl.ds(pl.multiple_of((1 - core) * HALF, HALF), HALF), :]
    for i in range(9):
        at = slice(i * 3 * C, (i + 1) * 3 * C)
        send_ref[at, :] = nt(stack_ref[at, :], other).astype(BF)
    send_ref[ROWS:ROWSP, :] = jnp.zeros((ROWSP - ROWS, HALF), BF)


def keep_body(act, ids, own_ref, oth_ref, both_ref, got_ref, keep_ref, *refs):
    send_refs, (stack_ref, full_ref) = refs[:3], refs[3:]
    sy, core, chip = ids[1], ids[2], ids[3]
    take(both_ref, 0 if act else 1, full_ref)
    fill_windows(own_ref, oth_ref, stack_ref, sy, not act, act)
    stack_ref[ROWS:ROWSP, :] = jnp.zeros((ROWSP - ROWS, NXL * SLAB), BF)
    mine = full_ref[pl.ds(pl.multiple_of(core * HALF, HALF), HALF), :]
    for k in (1, 3, 2, 0):
        for part in range(2):
            n = BLOCK // 2 - 8 * (1 - 2 * part)
            first = part * 160
            at = pl.ds(pl.multiple_of(((chip + k) % 4) * BLOCK + first, 16), n)
            total = nt(stack_ref[at, :], mine) + got_ref[at, :].astype(F32)
            to = slice(first, first + n)
            if k == 0:
                keep_ref[to, :] = total
            else:
                send_refs[k - 1][to, :] = total.astype(BF)


def data_body(ids, *refs):
    own_ref, oth_ref, w_ref, out_ref, stack_ref = refs
    fill_windows(own_ref, oth_ref, stack_ref, ids[1], True, False)
    for i in range(3):
        out_ref[i * 256 : (i + 1) * 256, :] = jnp.dot(
            w_ref[i * 256 : (i + 1) * 256, :], stack_ref[...], preferred_element_type=F32
        ).astype(BF)


def to_side(dx, flip):
    return [
        (sx * 2 + sy, (sx + dx) * 2 + (1 - sy if flip else sy))
        for sx in range(4)
        for sy in range(2)
        if 0 <= sx + dx < 4
    ]


def halo(whole):
    send = functools.partial(lax.ppermute, axis_name=LINE)
    first, last = whole[:, :SLAB], whole[:, whole.shape[1] - SLAB :]
    sides = []
    for flip, mid in ((False, whole), (True, send(whole, perm=to_side(0, True)))):
        left = send(last, perm=to_side(1, flip))
        right = send(first, perm=to_side(-1, flip))
        sides.append(jnp.concatenate([left, mid, right], axis=1))
    return tuple(sides)


def to_all(x, axis, count):
    many = jnp.broadcast_to(x[None], (count,) + x.shape)
    return lax.all_to_all(many, axis, 0, 0, tiled=True)


def along(shift):
    return [(place(x, c), place((x + shift) % 4, c)) for x in range(4) for c in range(2)]


def filter_sums(ids, own, oth, both, act):
    n_pos = NXL * SLAB
    field = pltpu.VMEM((CH, n_pos), BF)
    sent = jax.ShapeDtypeStruct((ROWSP, HALF), BF)
    outs = [jax.ShapeDtypeStruct((BLOCK, HALF), F32)]
    outs += [jax.ShapeDtypeStruct((BLOCK, HALF), BF)] * 3

    def send():
        scratch = [pltpu.VMEM((ROWS, n_pos), BF), field]
        return call(functools.partial(send_body, act), sent, scratch, 3)(ids, own, oth, both)

    def keep(got):
        scratch = [pltpu.VMEM((ROWSP, n_pos), BF), field]
        body = functools.partial(keep_body, act)
        return call(body, tuple(outs), scratch, 4)(ids, own, oth, both, got)

    return send, keep


def arrive(split):
    own, one, two, three = split
    return [own] + [lax.ppermute(v, LINE, along(k)) for k, v in ((1, one), (3, three), (2, two))]


def line_sum(parts, factor, after=None):
    if after is not None:
        parts, _ = lax.optimization_barrier((parts, after))
    total = parts[0]
    for v in parts[1:]:
        total = total + v.astype(F32)
    return (total * factor).astype(BF)


def line_spread(block, after=None):
    got = {k: lax.ppermute(block, LINE, along(k)) for k in (1, 3, 2)}
    if after is not None:
        got, _ = lax.optimization_barrier((got, after))
    mine = jnp.concatenate([block, got[1], got[2], got[3]], axis=0)
    return mine, lax.ppermute(mine, LINE, OTHER_CORE)


def write_body(ids, mine_ref, other_ref, out_ref):
    core = ids[2]
    mine = mine_ref[0].astype(F32)
    other = other_ref[0].astype(F32)
    out_ref[:, :, :HALF] = jnp.where(core == 0, mine, other)
    out_ref[:, :, HALF:] = jnp.where(core == 0, other, mine)


def write(ids, mine, other):
    shape = (4, OFFP // 4, C, HALF)
    spec = pl.BlockSpec((1,) + shape[1:], lambda i, ids: ((ids[3] + 4 - i) % 4, 0, 0, 0))
    return pl.pallas_call(
        write_body,
        out_shape=jax.ShapeDtypeStruct((OFF, C, CH), F32),
        grid_spec=pltpu.PrefetchScalarGridSpec(
            num_scalar_prefetch=1,
            grid=(4,),
            in_specs=[spec, spec],
            out_specs=pl.BlockSpec((OFFP // 4, C, CH), lambda i, ids: (i, 0, 0)),
        ),
        compiler_params=pltpu.CompilerParams(vmem_limit_bytes=32 << 20),
    )(ids, mine.reshape(shape), other.reshape(shape))


def shards(inputs, pre_act, out_grad, weight_one, weight_two):
    shape = pre_act.shape
    sx, sy = lax.axis_index("sx"), lax.axis_index("sy")
    core = sx % 2
    chip = sx // 2 + 2 * sy
    ids = jnp.stack([sx, sy, core, chip]).astype(jnp.int32)
    n_pos = NXL * SLAB
    factor = 1.0 / 64.0
    wide = n_pos + 2 * SLAB
    wide_f = jax.ShapeDtypeStruct((C, wide), F32)
    wide_b = jax.ShapeDtypeStruct((C, wide), BF)
    mid_f = jax.ShapeDtypeStruct((C, n_pos), F32)

    both = jnp.concatenate([out_grad.reshape(C, n_pos), inputs.reshape(C, n_pos)], axis=0)
    both = to_all(both, "ch", 16)
    pre = halo(pre_act.reshape(C, n_pos))
    w_two = weight_two.reshape(ROWS, CH)
    w_one = weight_one.reshape(ROWS, CH).T
    both, w_one, pre = lax.optimization_barrier((both, w_one, pre))

    own, over, pack = call(
        act_grad_body,
        (wide_f, wide_f, wide_f),
        [pltpu.VMEM((CH, n_pos), BF), pltpu.VMEM((3, 3 * C, wide), F32)],
        2,
    )(ids, w_two, both)
    pack = lax.ppermute(pack, LINE, to_side(0, True))

    send_two, keep_two = filter_sums(ids, *pre, both, True)
    send2 = send_two()
    pack, send2 = lax.optimization_barrier((pack, send2))
    got2 = lax.ppermute(send2, LINE, OTHER_CORE)
    own, oth, left, right = call(join_y_body, (wide_f, wide_f, mid_f, mid_f), [], 3)(
        ids, own, over, pack
    )
    from_left = lax.ppermute(right, LINE, to_side(1, False))
    from_right = lax.ppermute(left, LINE, to_side(-1, False))
    split2 = keep_two(got2)
    from_left, from_right, _ = lax.optimization_barrier((from_left, from_right, split2))
    delta = call(delta_body, (wide_b, wide_b), [], 6)(
        ids, own, oth, from_left, from_right, *pre
    )

    arrive2 = arrive(split2)
    send_one, keep_one = filter_sums(ids, *delta, both, False)
    got1 = lax.ppermute(send_one(), LINE, OTHER_CORE)
    split1 = keep_one(got1)
    delta, _ = lax.optimization_barrier((delta, split1))
    terms = call(
        data_body,
        jax.ShapeDtypeStruct((CH, n_pos), BF),
        [pltpu.VMEM((ROWS, n_pos), BF)],
        3,
    )(ids, *delta, w_one)
    got = lax.all_to_all(terms.reshape(16, C, n_pos), "ch", 0, 0, tiled=True)
    block2 = line_sum(arrive2, factor)
    block1 = line_sum(arrive(split1), factor, terms)
    filter_two = write(ids, *line_spread(block2, block1))
    input_grad = got.astype(F32).sum(axis=0).astype(BF).reshape(shape)
    filter_one = write(ids, *line_spread(block1, (filter_two, input_grad)))
    return input_grad, filter_one, filter_two


def solution(mesh):
    field = P("ch", "sx", "sy", None)
    filt = P(None, "ch", None)
    return jax.shard_map(
        shards,
        mesh=mesh,
        in_specs=(field, field, field, filt, filt),
        out_specs=(field, filt, filt),
        check_vma=False,
    )
```

```python
import functools

import jax
import jax.numpy as jnp
from jax import lax
from jax.experimental import pallas as pl
from jax.experimental.pallas import tpu as pltpu
from jax.sharding import PartitionSpec as P

BF = jnp.bfloat16
F32 = jnp.float32
LINE = ("sx", "sy")
OFF = 27
OFFP = 28
C = 48
CH = 768
SLAB = 128
NXL = 4
ROWS = OFF * C
ROWSP = OFFP * C
HALF = CH // 2
BLOCK = ROWSP // 4


def place(chip, core):
    return ((chip % 2) * 2 + core) * 2 + chip // 2


OTHER_CORE = [(place(x, c), place(x, 1 - c)) for x in range(4) for c in range(2)]


def vmem():
    return pl.BlockSpec(memory_space=pltpu.VMEM)


def smem():
    return pl.BlockSpec(memory_space=pltpu.SMEM)


def call(body, outs, scratch, n_in, us=1, limit=16):
    cost = pl.CostEstimate(flops=us * 10**9, transcendentals=0, bytes_accessed=us * 3 * 10**6)
    return pl.pallas_call(
        body,
        cost_estimate=cost,
        out_shape=outs,
        in_specs=[smem()] + [vmem()] * n_in,
        out_specs=jax.tree.map(lambda _: vmem(), outs),
        scratch_shapes=scratch,
        compiler_params=pltpu.CompilerParams(vmem_limit_bytes=limit << 20),
    )


def lanes():
    return lax.broadcasted_iota(jnp.int32, (C, SLAB), 1)


def shift_z(part, c, lane):
    if c == 1:
        return part
    z = lane % 64
    if c == 0:
        return jnp.where(z >= 1, pltpu.roll(part, 1, 1), 0.0)
    return jnp.where(z <= 62, pltpu.roll(part, SLAB - 1, 1), 0.0)


def fill_windows(own_ref, oth_ref, stack_ref, sy, mirror, act):
    lane = lanes()
    low = lane < 64
    for xp in range(NXL + 2):
        at = slice(xp * SLAB, (xp + 1) * SLAB)
        own, oth = own_ref[:, at].astype(F32), oth_ref[:, at].astype(F32)
        if act:
            own, oth = jnp.maximum(own, 0.0), jnp.maximum(oth, 0.0)
        r_own, r_oth = pltpu.roll(own, 64, 1), pltpu.roll(oth, 64, 1)
        rows = (
            jnp.where(low, jnp.where(sy == 1, r_oth, 0.0), r_own),
            own,
            jnp.where(low, r_own, jnp.where(sy == 0, r_oth, 0.0)),
        )
        for b in range(3):
            for c in range(3):
                part = shift_z(rows[b], c, lane).astype(BF)
                for a in range(3):
                    xl = xp - a
                    if 0 <= xl < NXL:
                        o = 9 * a + 3 * b + c
                        o = 26 - o if mirror else o
                        stack_ref[o * C : (o + 1) * C, xl * SLAB : (xl + 1) * SLAB] = part


def line_windows(line_ref, stack_ref, first, sx, sy):
    lane = lanes()
    low = lane < 64
    for xp in range(NXL + 2):
        peer_x = sx + (-1 if xp == 0 else 1 if xp == NXL + 1 else 0)
        inside = jnp.logical_and(peer_x >= 0, peer_x <= 3)
        peer_x = jnp.clip(peer_x, 0, 3)
        at = ((xp - 1) % NXL) * SLAB
        own = line_ref[peer_x * 2 + sy, :, at : at + SLAB].astype(F32)
        oth = line_ref[peer_x * 2 + 1 - sy, :, at : at + SLAB].astype(F32)
        if xp in (0, NXL + 1):
            own, oth = jnp.where(inside, own, 0.0), jnp.where(inside, oth, 0.0)
        r_own, r_oth = pltpu.roll(own, 64, 1), pltpu.roll(oth, 64, 1)
        rows = (
            jnp.where(low, jnp.where(sy == 1, r_oth, 0.0), r_own),
            own,
            jnp.where(low, r_own, jnp.where(sy == 0, r_oth, 0.0)),
        )
        for b in range(3):
            for c in range(3):
                part = shift_z(rows[b], c, lane).astype(BF)
                for a in range(3):
                    xl = xp - a
                    if 0 <= xl < NXL:
                        o = 26 - (9 * a + 3 * b + c)
                        to = first + xl * SLAB
                        stack_ref[o * C : (o + 1) * C, to : to + SLAB] = part


def nt(left, right):
    return lax.dot_general(left, right, (((1,), (1,)), ((), ())), preferred_element_type=F32)


def take(grad_ref, field_ref):
    for k in range(16):
        field_ref[k * C : (k + 1) * C, :] = grad_ref[k]


def act_grad_body(ids, w_ref, grad_ref, own_ref, over_ref, pack_ref, field_ref, u_ref):
    sy = ids[1]
    take(grad_ref, field_ref)
    grad = field_ref[...]
    u_ref[...] = jnp.zeros_like(u_ref)
    for a in range(3):
        for b in range(3):
            o = 9 * a + 3 * b
            y = jnp.dot(w_ref[o * C : (o + 3) * C, :], grad, preferred_element_type=F32)
            u_ref[b, :, a * SLAB : (a + NXL) * SLAB] += y
    lane = lanes()
    low = lane < 64
    for xp in range(NXL + 2):
        at = slice(xp * SLAB, (xp + 1) * SLAB)
        v = [
            sum(shift_z(u_ref[b, c * C : (c + 1) * C, at], 2 - c, lane) for c in range(3))
            for b in range(3)
        ]
        r0, r2 = pltpu.roll(v[0], 64, 1), pltpu.roll(v[2], 64, 1)
        own = v[1] + jnp.where(low, r0, r2)
        over = jnp.where(sy == 0, jnp.where(low, r2, 0.0), jnp.where(low, 0.0, r0))
        own_ref[:, at], over_ref[:, at] = own, over
        pack_ref[:, at] = jnp.where(low, jnp.where(sy == 0, over, own), jnp.where(sy == 0, own, over))


def join_y_body(ids, own_ref, over_ref, pack_ref, own_out, oth_out, left_out, right_out):
    sy = ids[1]
    low = lanes() < 64
    for xp in range(NXL + 2):
        at = slice(xp * SLAB, (xp + 1) * SLAB)
        pack = pack_ref[:, at]
        lower, upper = jnp.where(low, pack, 0.0), jnp.where(low, 0.0, pack)
        own = own_ref[:, at] + jnp.where(sy == 0, upper, lower)
        oth = over_ref[:, at] + jnp.where(sy == 0, lower, upper)
        own_out[:, at], oth_out[:, at] = own, oth
        for out, first in ((left_out, 0), (right_out, NXL)):
            if first <= xp < first + 2:
                k = (xp - first) * SLAB
                out[:, k : k + SLAB] = own
                out[:, k + 2 * SLAB : k + 3 * SLAB] = oth


def delta_body(ids, own_ref, oth_ref, left_ref, right_ref, pre_own_ref, pre_oth_ref, *outs):
    own_out, oth_out, mid_out = outs
    for xp in range(NXL + 2):
        at = slice(xp * SLAB, (xp + 1) * SLAB)
        for grad_ref, pre_ref, out, half in (
            (own_ref, pre_own_ref, own_out, 0),
            (oth_ref, pre_oth_ref, oth_out, 2 * SLAB),
        ):
            grad = grad_ref[:, at]
            if xp < 2:
                k = half + xp * SLAB
                grad = grad + left_ref[:, k : k + SLAB]
            if xp >= NXL:
                k = half + (xp - NXL) * SLAB
                grad = grad + right_ref[:, k : k + SLAB]
            delta = jnp.where(pre_ref[:, at].astype(F32) > 0, grad, 0.0).astype(BF)
            out[:, at] = delta
            if half == 0 and 1 <= xp <= NXL:
                mid_out[:, (xp - 1) * SLAB : xp * SLAB] = delta


def send_body(ids, own_ref, oth_ref, grad_ref, send_ref, stack_ref, full_ref):
    sy, core = ids[1], ids[2]
    take(grad_ref, full_ref)
    fill_windows(own_ref, oth_ref, stack_ref, sy, False, True)
    other = full_ref[pl.ds(pl.multiple_of((1 - core) * HALF, HALF), HALF), :]
    for i in range(9):
        at = slice(i * 3 * C, (i + 1) * 3 * C)
        send_ref[at, :] = nt(stack_ref[at, :], other).astype(BF)
    send_ref[ROWS:ROWSP, :] = jnp.zeros((ROWSP - ROWS, HALF), BF)


def keep_body(ids, own_ref, oth_ref, grad_ref, got_ref, keep_ref, *refs):
    send_refs, (stack_ref, full_ref) = refs[:3], refs[3:]
    sy, core, chip = ids[1], ids[2], ids[3]
    take(grad_ref, full_ref)
    fill_windows(own_ref, oth_ref, stack_ref, sy, False, True)
    stack_ref[ROWS:ROWSP, :] = jnp.zeros((ROWSP - ROWS, NXL * SLAB), BF)
    mine = full_ref[pl.ds(pl.multiple_of(core * HALF, HALF), HALF), :]
    for k in (1, 3, 2, 0):
        for part in range(2):
            n = BLOCK // 2 - 8 * (1 - 2 * part)
            first = part * 160
            at = pl.ds(pl.multiple_of(((chip + k) % 4) * BLOCK + first, 16), n)
            total = nt(stack_ref[at, :], mine) + got_ref[at, :].astype(F32)
            to = slice(first, first + n)
            if k == 0:
                keep_ref[to, :] = total
            else:
                send_refs[k - 1][to, :] = total.astype(BF)


PART = 4
CHALF = C // 2


def whole_body(first, ids, line_ref, in_ref, *refs):
    if first == 0:
        out_ref, field_ref, stack_ref, full_ref = refs
        acc_ref = out_ref
    else:
        before_ref, out_ref, field_ref, stack_ref, full_ref, acc_ref = refs
    core, chip = ids[2], ids[3]

    def where_is(r):
        chip_r = (chip + 4 - r // 2) % 4
        core_r = core if r % 2 == 0 else 1 - core
        return (chip_r % 2) * 2 + core_r, chip_r // 2

    for r in range(8):
        sx, sy = where_is(r)
        field_ref[sx * 2 + sy] = line_ref[r]
    for half in range(PART // 2):
        for j in range(2):
            r = half * 2 + j
            line_windows(field_ref, stack_ref, j * NXL * SLAB, *where_is(first + r))
            at = slice(j * NXL * SLAB, (j + 1) * NXL * SLAB)
            for k in range(8):
                pair = [in_ref[2 * k + i, r].astype(F32) for i in range(2)]
                full_ref[k * C : (k + 1) * C, at] = jnp.concatenate(pair, axis=0).astype(BF)
        for i in range(9):
            at = slice(i * 3 * C, (i + 1) * 3 * C)
            total = nt(stack_ref[at, :], full_ref[...])
            if half > 0:
                total = total + acc_ref[at, :]
            elif first > 0:
                total = total + before_ref[at, :]
            if first > 0 and half == PART // 2 - 1:
                out_ref[at, :] = (total * (1.0 / 64.0)).astype(BF)
            else:
                acc_ref[at, :] = total


def whole(ids, first, line, fields, before=None):
    n = 2 * NXL * SLAB
    scratch = [
        pltpu.VMEM((8, C, NXL * SLAB), BF),
        pltpu.VMEM((ROWS, n), BF),
        pltpu.VMEM((HALF, n), BF),
    ]
    args = (ids, line, fields)
    out = jax.ShapeDtypeStruct((ROWS, HALF), F32)
    if before is not None:
        args += (before,)
        out = jax.ShapeDtypeStruct((ROWS, HALF), BF)
        scratch.append(pltpu.VMEM((ROWS, HALF), F32))
    return call(functools.partial(whole_body, first), out, scratch, len(args) - 1, 7)(*args)


def merge_body(ids, mine_ref, other_ref, out_ref, order_ref):
    @pl.when(pl.program_id(0) == 0)
    def _():
        row = lax.broadcasted_iota(jnp.int32, (HALF, CH), 0)
        col = lax.broadcasted_iota(jnp.int32, (HALF, CH), 1)
        at = row + CHALF * (row // CHALF)
        for half in range(2):
            order_ref[half] = jnp.where(col == at + CHALF * half, 1.0, 0.0).astype(BF)

    core = ids[2]
    out = jnp.dot(mine_ref[...], order_ref[core], preferred_element_type=F32)
    out += jnp.dot(other_ref[...], order_ref[1 - core], preferred_element_type=F32)
    for i in range(3):
        out_ref[i] = out[i * C : (i + 1) * C, :]


def merge(ids, mine, other):
    spec = pl.BlockSpec((3 * C, HALF), lambda i, ids: (i, 0))
    return pl.pallas_call(
        merge_body,
        out_shape=jax.ShapeDtypeStruct((OFF, C, CH), F32),
        grid_spec=pltpu.PrefetchScalarGridSpec(
            num_scalar_prefetch=1,
            grid=(9,),
            in_specs=[spec, spec],
            out_specs=pl.BlockSpec((3, C, CH), lambda i, ids: (i, 0, 0)),
            scratch_shapes=[pltpu.VMEM((2, HALF, CH), BF)],
        ),
        compiler_params=pltpu.CompilerParams(vmem_limit_bytes=16 << 20),
    )(ids, mine, other)


def gather_line(mine, other):
    pair = jnp.stack([mine, other])
    got = {k: lax.ppermute(pair, LINE, along(k)) for k in (1, 3, 2)}
    return jnp.concatenate([pair, got[1], got[2], got[3]], axis=0)


def data_body(ids, *refs):
    own_ref, oth_ref, w_ref, out_ref, stack_ref = refs
    fill_windows(own_ref, oth_ref, stack_ref, ids[1], True, False)
    for i in range(3):
        out_ref[i * 256 : (i + 1) * 256, :] = jnp.dot(
            w_ref[i * 256 : (i + 1) * 256, :], stack_ref[...], preferred_element_type=F32
        ).astype(BF)


def to_side(dx, flip):
    return [
        (sx * 2 + sy, (sx + dx) * 2 + (1 - sy if flip else sy))
        for sx in range(4)
        for sy in range(2)
        if 0 <= sx + dx < 4
    ]


def halo(whole):
    send = functools.partial(lax.ppermute, axis_name=LINE)
    first, last = whole[:, :SLAB], whole[:, whole.shape[1] - SLAB :]
    sides = []
    for flip, mid in ((False, whole), (True, send(whole, perm=to_side(0, True)))):
        left = send(last, perm=to_side(1, flip))
        right = send(first, perm=to_side(-1, flip))
        sides.append(jnp.concatenate([left, mid, right], axis=1))
    return tuple(sides)


def to_all(x, axis, count):
    many = jnp.broadcast_to(x[None], (count,) + x.shape)
    return lax.all_to_all(many, axis, 0, 0, tiled=True)


def along(shift):
    return [(place(x, c), place((x + shift) % 4, c)) for x in range(4) for c in range(2)]


def filter_sums(ids, own, oth, grad):
    n_pos = NXL * SLAB
    field = pltpu.VMEM((CH, n_pos), BF)
    sent = jax.ShapeDtypeStruct((ROWSP, HALF), BF)
    outs = [jax.ShapeDtypeStruct((BLOCK, HALF), F32)]
    outs += [jax.ShapeDtypeStruct((BLOCK, HALF), BF)] * 3

    def send():
        scratch = [pltpu.VMEM((ROWS, n_pos), BF), field]
        return call(send_body, sent, scratch, 3, 2)(ids, own, oth, grad)

    def keep(got):
        scratch = [pltpu.VMEM((ROWSP, n_pos), BF), field]
        return call(keep_body, tuple(outs), scratch, 4, 2)(ids, own, oth, grad, got)

    return send, keep


def arrive(split):
    own, one, two, three = split
    return [own] + [lax.ppermute(v, LINE, along(k)) for k, v in ((1, one), (3, three), (2, two))]


def line_sum(parts, factor, after=None):
    if after is not None:
        parts, _ = lax.optimization_barrier((parts, after))
    total = parts[0]
    for v in parts[1:]:
        total = total + v.astype(F32)
    return (total * factor).astype(BF)


def line_spread(block, after=None):
    got = {k: lax.ppermute(block, LINE, along(k)) for k in (1, 3, 2)}
    if after is not None:
        got, _ = lax.optimization_barrier((got, after))
    mine = jnp.concatenate([block, got[1], got[2], got[3]], axis=0)
    return mine, lax.ppermute(mine, LINE, OTHER_CORE)


def write_body(ids, mine_ref, other_ref, out_ref):
    core = ids[2]
    mine = mine_ref[0].astype(F32)
    other = other_ref[0].astype(F32)
    out_ref[:, :, :HALF] = jnp.where(core == 0, mine, other)
    out_ref[:, :, HALF:] = jnp.where(core == 0, other, mine)


def write(ids, mine, other):
    shape = (4, OFFP // 4, C, HALF)
    spec = pl.BlockSpec((1,) + shape[1:], lambda i, ids: ((ids[3] + 4 - i) % 4, 0, 0, 0))
    return pl.pallas_call(
        write_body,
        out_shape=jax.ShapeDtypeStruct((OFF, C, CH), F32),
        grid_spec=pltpu.PrefetchScalarGridSpec(
            num_scalar_prefetch=1,
            grid=(4,),
            in_specs=[spec, spec],
            out_specs=pl.BlockSpec((OFFP // 4, C, CH), lambda i, ids: (i, 0, 0)),
        ),
        compiler_params=pltpu.CompilerParams(vmem_limit_bytes=32 << 20),
    )(ids, mine.reshape(shape), other.reshape(shape))


def shards(inputs, pre_act, out_grad, weight_one, weight_two):
    shape = pre_act.shape
    sx, sy = lax.axis_index("sx"), lax.axis_index("sy")
    core = sx % 2
    chip = sx // 2 + 2 * sy
    ids = jnp.stack([sx, sy, core, chip]).astype(jnp.int32)
    n_pos = NXL * SLAB
    factor = 1.0 / 64.0
    wide = n_pos + 2 * SLAB
    wide_f = jax.ShapeDtypeStruct((C, wide), F32)
    wide_b = jax.ShapeDtypeStruct((C, wide), BF)
    mid_f = jax.ShapeDtypeStruct((C, n_pos), F32)

    grad = to_all(out_grad.reshape(C, n_pos), "ch", 16)
    field = inputs.reshape(C, n_pos)
    lower, upper = field[:CHALF], field[CHALF:]
    other = lax.ppermute(jnp.where(core == 0, upper, lower), LINE, OTHER_CORE)
    line_in = gather_line(jnp.where(core == 0, lower, upper), other)
    pre_act, other = lax.optimization_barrier((pre_act, other))
    pre = halo(pre_act.reshape(C, n_pos))
    w_two = weight_two.reshape(ROWS, CH)
    grad, pre, line_in = lax.optimization_barrier((grad, pre, line_in))
    fields = [to_all(line_in[i : i + PART], "ch", 16) for i in (0, PART)]

    own, over, pack = call(
        act_grad_body,
        (wide_f, wide_f, wide_f),
        [pltpu.VMEM((CH, n_pos), BF), pltpu.VMEM((3, 3 * C, wide), F32)],
        2,
        2,
    )(ids, w_two, grad)
    pack = lax.ppermute(pack, LINE, to_side(0, True))

    send_two, keep_two = filter_sums(ids, *pre, grad)
    send2 = send_two()
    pack, send2 = lax.optimization_barrier((pack, send2))
    got2 = lax.ppermute(send2, LINE, OTHER_CORE)
    own, oth, left, right = call(join_y_body, (wide_f, wide_f, mid_f, mid_f), [], 3)(
        ids, own, over, pack
    )
    from_left = lax.ppermute(right, LINE, to_side(1, False))
    from_right = lax.ppermute(left, LINE, to_side(-1, False))
    got2, _ = lax.optimization_barrier((got2, left))
    split2 = keep_two(got2)
    from_left, from_right, fields[0], _ = lax.optimization_barrier(
        (from_left, from_right, fields[0], split2)
    )
    mid_b = jax.ShapeDtypeStruct((C, n_pos), BF)
    *delta, middle = call(delta_body, (wide_b, wide_b, mid_b), [], 6)(
        ids, own, oth, from_left, from_right, *pre
    )
    line = gather_line(middle, lax.ppermute(middle, LINE, OTHER_CORE))
    arrive2 = arrive(split2)
    weight_one, delta = lax.optimization_barrier((weight_one, delta))
    w_one = weight_one.reshape(ROWS, CH).T
    terms = call(
        data_body,
        jax.ShapeDtypeStruct((CH, n_pos), BF),
        [pltpu.VMEM((ROWS, n_pos), BF)],
        3,
        3,
    )(ids, *delta, w_one)
    part = whole(ids, 0, line, fields[0])
    part, terms = lax.optimization_barrier((part, terms))
    block2 = line_sum(arrive2, factor)
    mine1 = whole(ids, PART, line, fields[1], part)
    got = lax.all_to_all(terms.reshape(16, C, n_pos), "ch", 0, 0, tiled=True)
    filter_two = write(ids, *line_spread(block2))
    other1 = lax.ppermute(mine1, LINE, OTHER_CORE)
    other1, _, got = lax.optimization_barrier((other1, filter_two, got))
    filter_one = merge(ids, mine1, other1)
    input_grad = got.astype(F32).sum(axis=0).astype(BF).reshape(shape)
    return input_grad, filter_one, filter_two


def solution(mesh):
    field = P("ch", "sx", "sy", None)
    filt = P(None, "ch", None)
    return jax.shard_map(
        shards,
        mesh=mesh,
        in_specs=(field, field, field, filt, filt),
        out_specs=(field, filt, filt),
        check_vma=False,
    )
```

```python
import functools

import jax
import jax.numpy as jnp
from jax import lax
from jax.experimental import pallas as pl
from jax.experimental.pallas import tpu as pltpu
from jax.sharding import PartitionSpec as P

BF = jnp.bfloat16
F32 = jnp.float32
LINE = ("sx", "sy")
OFF = 27
OFFP = 28
C = 48
CH = 768
SLAB = 128
NXL = 4
ROWS = OFF * C
ROWSP = OFFP * C
HALF = CH // 2
BLOCK = ROWSP // 4


def place(chip, core):
    return ((chip % 2) * 2 + core) * 2 + chip // 2


OTHER_CORE = [(place(x, c), place(x, 1 - c)) for x in range(4) for c in range(2)]


def vmem():
    return pl.BlockSpec(memory_space=pltpu.VMEM)


def smem():
    return pl.BlockSpec(memory_space=pltpu.SMEM)


def call(body, outs, scratch, n_in, limit=16):
    return pl.pallas_call(
        body,
        out_shape=outs,
        in_specs=[smem()] + [vmem()] * n_in,
        out_specs=jax.tree.map(lambda _: vmem(), outs),
        scratch_shapes=scratch,
        compiler_params=pltpu.CompilerParams(vmem_limit_bytes=limit << 20),
    )


def lanes():
    return lax.broadcasted_iota(jnp.int32, (C, SLAB), 1)


def shift_z(part, c, lane):
    if c == 1:
        return part
    z = lane % 64
    if c == 0:
        return jnp.where(z >= 1, pltpu.roll(part, 1, 1), 0.0)
    return jnp.where(z <= 62, pltpu.roll(part, SLAB - 1, 1), 0.0)


def fill_windows(own_ref, oth_ref, stack_ref, sy, mirror, act):
    lane = lanes()
    low = lane < 64
    for xp in range(NXL + 2):
        at = slice(xp * SLAB, (xp + 1) * SLAB)
        own, oth = own_ref[:, at].astype(F32), oth_ref[:, at].astype(F32)
        if act:
            own, oth = jnp.maximum(own, 0.0), jnp.maximum(oth, 0.0)
        r_own, r_oth = pltpu.roll(own, 64, 1), pltpu.roll(oth, 64, 1)
        rows = (
            jnp.where(low, jnp.where(sy == 1, r_oth, 0.0), r_own),
            own,
            jnp.where(low, r_own, jnp.where(sy == 0, r_oth, 0.0)),
        )
        for b in range(3):
            for c in range(3):
                part = shift_z(rows[b], c, lane).astype(BF)
                for a in range(3):
                    xl = xp - a
                    if 0 <= xl < NXL:
                        o = 9 * a + 3 * b + c
                        o = 26 - o if mirror else o
                        stack_ref[o * C : (o + 1) * C, xl * SLAB : (xl + 1) * SLAB] = part


def nt(left, right):
    return lax.dot_general(left, right, (((1,), (1,)), ((), ())), preferred_element_type=F32)


def take(both_ref, second, field_ref):
    for k in range(16):
        field_ref[k * C : (k + 1) * C, :] = both_ref[k, second * C : (second + 1) * C, :]


def act_grad_body(ids, w_ref, both_ref, own_ref, over_ref, pack_ref, field_ref, u_ref):
    sy = ids[1]
    take(both_ref, 0, field_ref)
    grad = field_ref[...]
    u_ref[...] = jnp.zeros_like(u_ref)
    for a in range(3):
        for b in range(3):
            o = 9 * a + 3 * b
            y = jnp.dot(w_ref[o * C : (o + 3) * C, :], grad, preferred_element_type=F32)
            u_ref[b, :, a * SLAB : (a + NXL) * SLAB] += y
    lane = lanes()
    low = lane < 64
    for xp in range(NXL + 2):
        at = slice(xp * SLAB, (xp + 1) * SLAB)
        v = [
            sum(shift_z(u_ref[b, c * C : (c + 1) * C, at], 2 - c, lane) for c in range(3))
            for b in range(3)
        ]
        r0, r2 = pltpu.roll(v[0], 64, 1), pltpu.roll(v[2], 64, 1)
        own = v[1] + jnp.where(low, r0, r2)
        over = jnp.where(sy == 0, jnp.where(low, r2, 0.0), jnp.where(low, 0.0, r0))
        own_ref[:, at], over_ref[:, at] = own, over
        pack_ref[:, at] = jnp.where(low, jnp.where(sy == 0, over, own), jnp.where(sy == 0, own, over))


def join_y_body(ids, own_ref, over_ref, pack_ref, own_out, oth_out, left_out, right_out):
    sy = ids[1]
    low = lanes() < 64
    for xp in range(NXL + 2):
        at = slice(xp * SLAB, (xp + 1) * SLAB)
        pack = pack_ref[:, at]
        lower, upper = jnp.where(low, pack, 0.0), jnp.where(low, 0.0, pack)
        own = own_ref[:, at] + jnp.where(sy == 0, upper, lower)
        oth = over_ref[:, at] + jnp.where(sy == 0, lower, upper)
        own_out[:, at], oth_out[:, at] = own, oth
        for out, first in ((left_out, 0), (right_out, NXL)):
            if first <= xp < first + 2:
                k = (xp - first) * SLAB
                out[:, k : k + SLAB] = own
                out[:, k + 2 * SLAB : k + 3 * SLAB] = oth


def delta_body(ids, own_ref, oth_ref, left_ref, right_ref, pre_own_ref, pre_oth_ref, own_out, oth_out):
    for xp in range(NXL + 2):
        at = slice(xp * SLAB, (xp + 1) * SLAB)
        for grad_ref, pre_ref, out, half in (
            (own_ref, pre_own_ref, own_out, 0),
            (oth_ref, pre_oth_ref, oth_out, 2 * SLAB),
        ):
            grad = grad_ref[:, at]
            if xp < 2:
                k = half + xp * SLAB
                grad = grad + left_ref[:, k : k + SLAB]
            if xp >= NXL:
                k = half + (xp - NXL) * SLAB
                grad = grad + right_ref[:, k : k + SLAB]
            out[:, at] = jnp.where(pre_ref[:, at].astype(F32) > 0, grad, 0.0).astype(BF)


def send_body(act, ids, own_ref, oth_ref, both_ref, send_ref, stack_ref, full_ref):
    sy, core = ids[1], ids[2]
    take(both_ref, 0 if act else 1, full_ref)
    fill_windows(own_ref, oth_ref, stack_ref, sy, not act, act)
    other = full_ref[pl.ds(pl.multiple_of((1 - core) * HALF, HALF), HALF), :]
    for i in range(9):
        at = slice(i * 3 * C, (i + 1) * 3 * C)
        send_ref[at, :] = nt(stack_ref[at, :], other).astype(BF)
    send_ref[ROWS:ROWSP, :] = jnp.zeros((ROWSP - ROWS, HALF), BF)


def keep_body(act, ids, own_ref, oth_ref, both_ref, got_ref, keep_ref, *refs):
    send_refs, (stack_ref, full_ref) = refs[:3], refs[3:]
    sy, core, chip = ids[1], ids[2], ids[3]
    take(both_ref, 0 if act else 1, full_ref)
    fill_windows(own_ref, oth_ref, stack_ref, sy, not act, act)
    stack_ref[ROWS:ROWSP, :] = jnp.zeros((ROWSP - ROWS, NXL * SLAB), BF)
    mine = full_ref[pl.ds(pl.multiple_of(core * HALF, HALF), HALF), :]
    for k in (1, 3, 2, 0):
        for part in range(2):
            n = BLOCK // 2 - 8 * (1 - 2 * part)
            first = part * 160
            at = pl.ds(pl.multiple_of(((chip + k) % 4) * BLOCK + first, 16), n)
            total = nt(stack_ref[at, :], mine) + got_ref[at, :].astype(F32)
            to = slice(first, first + n)
            if k == 0:
                keep_ref[to, :] = total
            else:
                send_refs[k - 1][to, :] = total.astype(BF)


def data_body(ids, *refs):
    own_ref, oth_ref, w_ref, out_ref, stack_ref = refs
    fill_windows(own_ref, oth_ref, stack_ref, ids[1], True, False)
    for i in range(3):
        out_ref[i * 256 : (i + 1) * 256, :] = jnp.dot(
            w_ref[i * 256 : (i + 1) * 256, :], stack_ref[...], preferred_element_type=F32
        ).astype(BF)


def to_side(dx, flip):
    return [
        (sx * 2 + sy, (sx + dx) * 2 + (1 - sy if flip else sy))
        for sx in range(4)
        for sy in range(2)
        if 0 <= sx + dx < 4
    ]


def halo(whole):
    send = functools.partial(lax.ppermute, axis_name=LINE)
    first, last = whole[:, :SLAB], whole[:, whole.shape[1] - SLAB :]
    sides = []
    for flip, mid in ((False, whole), (True, send(whole, perm=to_side(0, True)))):
        left = send(last, perm=to_side(1, flip))
        right = send(first, perm=to_side(-1, flip))
        sides.append(jnp.concatenate([left, mid, right], axis=1))
    return tuple(sides)


def to_all(x, axis, count):
    many = jnp.broadcast_to(x[None], (count,) + x.shape)
    return lax.all_to_all(many, axis, 0, 0, tiled=True)


def along(shift):
    return [(place(x, c), place((x + shift) % 4, c)) for x in range(4) for c in range(2)]


def filter_sums(ids, own, oth, both, act):
    n_pos = NXL * SLAB
    field = pltpu.VMEM((CH, n_pos), BF)
    sent = jax.ShapeDtypeStruct((ROWSP, HALF), BF)
    outs = [jax.ShapeDtypeStruct((BLOCK, HALF), F32)]
    outs += [jax.ShapeDtypeStruct((BLOCK, HALF), BF)] * 3

    def send():
        scratch = [pltpu.VMEM((ROWS, n_pos), BF), field]
        return call(functools.partial(send_body, act), sent, scratch, 3)(ids, own, oth, both)

    def keep(got):
        scratch = [pltpu.VMEM((ROWSP, n_pos), BF), field]
        body = functools.partial(keep_body, act)
        return call(body, tuple(outs), scratch, 4)(ids, own, oth, both, got)

    return send, keep


def arrive(split):
    own, one, two, three = split
    return [own] + [lax.ppermute(v, LINE, along(k)) for k, v in ((1, one), (3, three), (2, two))]


def line_sum(parts, factor, after=None):
    if after is not None:
        parts, _ = lax.optimization_barrier((parts, after))
    total = parts[0]
    for v in parts[1:]:
        total = total + v.astype(F32)
    return (total * factor).astype(BF)


def line_send(block):
    return [block] + [lax.ppermute(block, LINE, along(k)) for k in (1, 3, 2)]


def line_join(parts, after):
    (own, one, three, two), _ = lax.optimization_barrier((parts, after))
    mine = jnp.concatenate([own, one, two, three], axis=0)
    return mine, lax.ppermute(mine, LINE, OTHER_CORE)


def write_body(ids, mine_ref, other_ref, out_ref):
    core = ids[2]
    mine = mine_ref[0].astype(F32)
    other = other_ref[0].astype(F32)
    out_ref[:, :, :HALF] = jnp.where(core == 0, mine, other)
    out_ref[:, :, HALF:] = jnp.where(core == 0, other, mine)


def write(ids, mine, other):
    shape = (4, OFFP // 4, C, HALF)
    spec = pl.BlockSpec((1,) + shape[1:], lambda i, ids: ((ids[3] + 4 - i) % 4, 0, 0, 0))
    return pl.pallas_call(
        write_body,
        out_shape=jax.ShapeDtypeStruct((OFF, C, CH), F32),
        grid_spec=pltpu.PrefetchScalarGridSpec(
            num_scalar_prefetch=1,
            grid=(4,),
            in_specs=[spec, spec],
            out_specs=pl.BlockSpec((OFFP // 4, C, CH), lambda i, ids: (i, 0, 0)),
        ),
        compiler_params=pltpu.CompilerParams(vmem_limit_bytes=32 << 20),
    )(ids, mine.reshape(shape), other.reshape(shape))


def shards(inputs, pre_act, out_grad, weight_one, weight_two):
    shape = pre_act.shape
    sx, sy = lax.axis_index("sx"), lax.axis_index("sy")
    core = sx % 2
    chip = sx // 2 + 2 * sy
    ids = jnp.stack([sx, sy, core, chip]).astype(jnp.int32)
    n_pos = NXL * SLAB
    factor = 1.0 / 64.0
    wide = n_pos + 2 * SLAB
    wide_f = jax.ShapeDtypeStruct((C, wide), F32)
    wide_b = jax.ShapeDtypeStruct((C, wide), BF)
    mid_f = jax.ShapeDtypeStruct((C, n_pos), F32)

    both = jnp.concatenate([out_grad.reshape(C, n_pos), inputs.reshape(C, n_pos)], axis=0)
    both = to_all(both, "ch", 16)
    pre = halo(pre_act.reshape(C, n_pos))
    w_two = weight_two.reshape(ROWS, CH)
    w_one = weight_one.reshape(ROWS, CH).T
    both, w_one, pre = lax.optimization_barrier((both, w_one, pre))

    own, over, pack = call(
        act_grad_body,
        (wide_f, wide_f, wide_f),
        [pltpu.VMEM((CH, n_pos), BF), pltpu.VMEM((3, 3 * C, wide), F32)],
        2,
    )(ids, w_two, both)
    pack = lax.ppermute(pack, LINE, to_side(0, True))

    send_two, keep_two = filter_sums(ids, *pre, both, True)
    send2 = send_two()
    pack, send2 = lax.optimization_barrier((pack, send2))
    got2 = lax.ppermute(send2, LINE, OTHER_CORE)
    own, oth, left, right = call(join_y_body, (wide_f, wide_f, mid_f, mid_f), [], 3)(
        ids, own, over, pack
    )
    from_left = lax.ppermute(right, LINE, to_side(1, False))
    from_right = lax.ppermute(left, LINE, to_side(-1, False))
    split2 = keep_two(got2)
    from_left, from_right, _ = lax.optimization_barrier((from_left, from_right, split2))
    delta = call(delta_body, (wide_b, wide_b), [], 6)(
        ids, own, oth, from_left, from_right, *pre
    )

    arrive2 = arrive(split2)
    send_one, keep_one = filter_sums(ids, *delta, both, False)
    got1 = lax.ppermute(send_one(), LINE, OTHER_CORE)
    split1 = keep_one(got1)
    arrive2, _ = lax.optimization_barrier((arrive2, split1))
    block2 = line_sum(arrive2, factor)
    delta, _ = lax.optimization_barrier((delta, block2))
    terms = call(
        data_body,
        jax.ShapeDtypeStruct((CH, n_pos), BF),
        [pltpu.VMEM((ROWS, n_pos), BF)],
        3,
    )(ids, *delta, w_one)
    got = lax.all_to_all(terms.reshape(16, C, n_pos), "ch", 0, 0, tiled=True)
    block1 = line_sum(arrive(split1), factor)
    spread2, spread1 = line_send(block2), line_send(block1)
    filter_two = write(ids, *line_join(spread2, (spread1[1], got)))
    input_grad = got.astype(F32).sum(axis=0).astype(BF).reshape(shape)
    filter_one = write(ids, *line_join(spread1, input_grad))
    return input_grad, filter_one, filter_two


def solution(mesh):
    field = P("ch", "sx", "sy", None)
    filt = P(None, "ch", None)
    return jax.shard_map(
        shards,
        mesh=mesh,
        in_specs=(field, field, field, filt, filt),
        out_specs=(field, filt, filt),
        check_vma=False,
    )
```

```python
import functools

import jax
import jax.numpy as jnp
from jax import lax
from jax.experimental import pallas as pl
from jax.experimental.pallas import tpu as pltpu
from jax.sharding import PartitionSpec as P

BF = jnp.bfloat16
F32 = jnp.float32
LINE = ("sx", "sy")
OFF = 27
OFFP = 28
C = 48
CH = 768
SLAB = 128
NXL = 4
ROWS = OFF * C
ROWSP = OFFP * C
HALF = CH // 2
BLOCK = ROWSP // 4


def place(chip, core):
    return ((chip % 2) * 2 + core) * 2 + chip // 2


OTHER_CORE = [(place(x, c), place(x, 1 - c)) for x in range(4) for c in range(2)]


def vmem():
    return pl.BlockSpec(memory_space=pltpu.VMEM)


def smem():
    return pl.BlockSpec(memory_space=pltpu.SMEM)


def call(body, outs, scratch, n_in, limit=16):
    return pl.pallas_call(
        body,
        out_shape=outs,
        in_specs=[smem()] + [vmem()] * n_in,
        out_specs=jax.tree.map(lambda _: vmem(), outs),
        scratch_shapes=scratch,
        compiler_params=pltpu.CompilerParams(vmem_limit_bytes=limit << 20),
    )


def lanes():
    return lax.broadcasted_iota(jnp.int32, (C, SLAB), 1)


def shift_z(part, c, lane):
    if c == 1:
        return part
    z = lane % 64
    if c == 0:
        return jnp.where(z >= 1, pltpu.roll(part, 1, 1), 0.0)
    return jnp.where(z <= 62, pltpu.roll(part, SLAB - 1, 1), 0.0)


def fill_windows(own_ref, oth_ref, stack_ref, sy, mirror, act):
    lane = lanes()
    low = lane < 64
    for xp in range(NXL + 2):
        at = slice(xp * SLAB, (xp + 1) * SLAB)
        own, oth = own_ref[:, at].astype(F32), oth_ref[:, at].astype(F32)
        if act:
            own, oth = jnp.maximum(own, 0.0), jnp.maximum(oth, 0.0)
        r_own, r_oth = pltpu.roll(own, 64, 1), pltpu.roll(oth, 64, 1)
        rows = (
            jnp.where(low, jnp.where(sy == 1, r_oth, 0.0), r_own),
            own,
            jnp.where(low, r_own, jnp.where(sy == 0, r_oth, 0.0)),
        )
        for b in range(3):
            for c in range(3):
                part = shift_z(rows[b], c, lane).astype(BF)
                for a in range(3):
                    xl = xp - a
                    if 0 <= xl < NXL:
                        o = 9 * a + 3 * b + c
                        o = 26 - o if mirror else o
                        stack_ref[o * C : (o + 1) * C, xl * SLAB : (xl + 1) * SLAB] = part


def nt(left, right):
    return lax.dot_general(left, right, (((1,), (1,)), ((), ())), preferred_element_type=F32)


def take(both_ref, second, field_ref):
    for k in range(16):
        field_ref[k * C : (k + 1) * C, :] = both_ref[k, second * C : (second + 1) * C, :]


def act_grad_body(ids, w_ref, both_ref, own_ref, over_ref, pack_ref, field_ref, u_ref):
    sy = ids[1]
    take(both_ref, 0, field_ref)
    grad = field_ref[...]
    u_ref[...] = jnp.zeros_like(u_ref)
    for a in range(3):
        for b in range(3):
            o = 9 * a + 3 * b
            y = jnp.dot(w_ref[o * C : (o + 3) * C, :], grad, preferred_element_type=F32)
            u_ref[b, :, a * SLAB : (a + NXL) * SLAB] += y
    lane = lanes()
    low = lane < 64
    for xp in range(NXL + 2):
        at = slice(xp * SLAB, (xp + 1) * SLAB)
        v = [
            sum(shift_z(u_ref[b, c * C : (c + 1) * C, at], 2 - c, lane) for c in range(3))
            for b in range(3)
        ]
        r0, r2 = pltpu.roll(v[0], 64, 1), pltpu.roll(v[2], 64, 1)
        own = v[1] + jnp.where(low, r0, r2)
        over = jnp.where(sy == 0, jnp.where(low, r2, 0.0), jnp.where(low, 0.0, r0))
        own_ref[:, at], over_ref[:, at] = own, over
        pack_ref[:, at] = jnp.where(low, jnp.where(sy == 0, over, own), jnp.where(sy == 0, own, over))


def join_y_body(ids, own_ref, over_ref, pack_ref, own_out, oth_out, left_out, right_out):
    sy = ids[1]
    low = lanes() < 64
    for xp in range(NXL + 2):
        at = slice(xp * SLAB, (xp + 1) * SLAB)
        pack = pack_ref[:, at]
        lower, upper = jnp.where(low, pack, 0.0), jnp.where(low, 0.0, pack)
        own = own_ref[:, at] + jnp.where(sy == 0, upper, lower)
        oth = over_ref[:, at] + jnp.where(sy == 0, lower, upper)
        own_out[:, at], oth_out[:, at] = own, oth
        for out, first in ((left_out, 0), (right_out, NXL)):
            if first <= xp < first + 2:
                k = (xp - first) * SLAB
                out[:, k : k + SLAB] = own
                out[:, k + 2 * SLAB : k + 3 * SLAB] = oth


def delta_body(ids, own_ref, oth_ref, left_ref, right_ref, pre_own_ref, pre_oth_ref, own_out, oth_out):
    for xp in range(NXL + 2):
        at = slice(xp * SLAB, (xp + 1) * SLAB)
        for grad_ref, pre_ref, out, half in (
            (own_ref, pre_own_ref, own_out, 0),
            (oth_ref, pre_oth_ref, oth_out, 2 * SLAB),
        ):
            grad = grad_ref[:, at]
            if xp < 2:
                k = half + xp * SLAB
                grad = grad + left_ref[:, k : k + SLAB]
            if xp >= NXL:
                k = half + (xp - NXL) * SLAB
                grad = grad + right_ref[:, k : k + SLAB]
            out[:, at] = jnp.where(pre_ref[:, at].astype(F32) > 0, grad, 0.0).astype(BF)


def send_body(act, ids, own_ref, oth_ref, both_ref, send_ref, stack_ref, full_ref):
    sy, core = ids[1], ids[2]
    take(both_ref, 0 if act else 1, full_ref)
    fill_windows(own_ref, oth_ref, stack_ref, sy, not act, act)
    other = full_ref[pl.ds(pl.multiple_of((1 - core) * HALF, HALF), HALF), :]
    for i in range(9):
        at = slice(i * 3 * C, (i + 1) * 3 * C)
        send_ref[at, :] = nt(stack_ref[at, :], other).astype(BF)
    send_ref[ROWS:ROWSP, :] = jnp.zeros((ROWSP - ROWS, HALF), BF)


def keep_body(act, ids, own_ref, oth_ref, both_ref, got_ref, keep_ref, *refs):
    send_refs, (stack_ref, full_ref) = refs[:3], refs[3:]
    sy, core, chip = ids[1], ids[2], ids[3]
    take(both_ref, 0 if act else 1, full_ref)
    fill_windows(own_ref, oth_ref, stack_ref, sy, not act, act)
    stack_ref[ROWS:ROWSP, :] = jnp.zeros((ROWSP - ROWS, NXL * SLAB), BF)
    mine = full_ref[pl.ds(pl.multiple_of(core * HALF, HALF), HALF), :]
    for k in (1, 3, 2, 0):
        for part in range(2):
            n = BLOCK // 2 - 8 * (1 - 2 * part)
            first = part * 160
            at = pl.ds(pl.multiple_of(((chip + k) % 4) * BLOCK + first, 16), n)
            total = nt(stack_ref[at, :], mine) + got_ref[at, :].astype(F32)
            to = slice(first, first + n)
            if k == 0:
                keep_ref[to, :] = total
            else:
                send_refs[k - 1][to, :] = total.astype(BF)


def data_body(ids, *refs):
    own_ref, oth_ref, w_ref, out_ref, stack_ref = refs
    fill_windows(own_ref, oth_ref, stack_ref, ids[1], True, False)
    for i in range(3):
        out_ref[i * 256 : (i + 1) * 256, :] = jnp.dot(
            w_ref[i * 256 : (i + 1) * 256, :], stack_ref[...], preferred_element_type=F32
        ).astype(BF)


def to_side(dx, flip):
    return [
        (sx * 2 + sy, (sx + dx) * 2 + (1 - sy if flip else sy))
        for sx in range(4)
        for sy in range(2)
        if 0 <= sx + dx < 4
    ]


def halo(whole):
    send = functools.partial(lax.ppermute, axis_name=LINE)
    first, last = whole[:, :SLAB], whole[:, whole.shape[1] - SLAB :]
    sides = []
    for flip, mid in ((False, whole), (True, send(whole, perm=to_side(0, True)))):
        left = send(last, perm=to_side(1, flip))
        right = send(first, perm=to_side(-1, flip))
        sides.append(jnp.concatenate([left, mid, right], axis=1))
    return tuple(sides)


def to_all(x, axis, count):
    many = jnp.broadcast_to(x[None], (count,) + x.shape)
    return lax.all_to_all(many, axis, 0, 0, tiled=True)


def along(shift):
    return [(place(x, c), place((x + shift) % 4, c)) for x in range(4) for c in range(2)]


def filter_sums(ids, own, oth, both, act):
    n_pos = NXL * SLAB
    field = pltpu.VMEM((CH, n_pos), BF)
    sent = jax.ShapeDtypeStruct((ROWSP, HALF), BF)
    outs = [jax.ShapeDtypeStruct((BLOCK, HALF), F32)]
    outs += [jax.ShapeDtypeStruct((BLOCK, HALF), BF)] * 3

    def send():
        scratch = [pltpu.VMEM((ROWS, n_pos), BF), field]
        return call(functools.partial(send_body, act), sent, scratch, 3)(ids, own, oth, both)

    def keep(got):
        scratch = [pltpu.VMEM((ROWSP, n_pos), BF), field]
        body = functools.partial(keep_body, act)
        return call(body, tuple(outs), scratch, 4)(ids, own, oth, both, got)

    return send, keep


def arrive(split):
    own, one, two, three = split
    return [own] + [lax.ppermute(v, LINE, along(k)) for k, v in ((1, one), (3, three), (2, two))]


def line_sum(parts, factor, after=None):
    if after is not None:
        parts, _ = lax.optimization_barrier((parts, after))
    total = parts[0]
    for v in parts[1:]:
        total = total + v.astype(F32)
    return (total * factor).astype(BF)


def line_send(block):
    return [block] + [lax.ppermute(block, LINE, along(k)) for k in (1, 3, 2)]


def line_join(parts, after):
    (own, one, three, two), _ = lax.optimization_barrier((parts, after))
    mine = jnp.concatenate([own, one, two, three], axis=0)
    return mine, lax.ppermute(mine, LINE, OTHER_CORE)


def write_body(ids, mine_ref, other_ref, out_ref):
    core = ids[2]
    for ref, half in ((mine_ref, core), (other_ref, 1 - core)):
        at = pl.ds(pl.multiple_of(half * HALF, HALF), HALF)
        out_ref[:, :, at] = ref[0].astype(F32)


def write(ids, mine, other):
    shape = (4, OFFP // 4, C, HALF)
    spec = pl.BlockSpec((1,) + shape[1:], lambda i, ids: ((ids[3] + 4 - i) % 4, 0, 0, 0))
    return pl.pallas_call(
        write_body,
        out_shape=jax.ShapeDtypeStruct((OFF, C, CH), F32),
        grid_spec=pltpu.PrefetchScalarGridSpec(
            num_scalar_prefetch=1,
            grid=(4,),
            in_specs=[spec, spec],
            out_specs=pl.BlockSpec((OFFP // 4, C, CH), lambda i, ids: (i, 0, 0)),
        ),
        compiler_params=pltpu.CompilerParams(vmem_limit_bytes=32 << 20),
    )(ids, mine.reshape(shape), other.reshape(shape))


def shards(inputs, pre_act, out_grad, weight_one, weight_two):
    shape = pre_act.shape
    sx, sy = lax.axis_index("sx"), lax.axis_index("sy")
    core = sx % 2
    chip = sx // 2 + 2 * sy
    ids = jnp.stack([sx, sy, core, chip]).astype(jnp.int32)
    n_pos = NXL * SLAB
    factor = 1.0 / 64.0
    wide = n_pos + 2 * SLAB
    wide_f = jax.ShapeDtypeStruct((C, wide), F32)
    wide_b = jax.ShapeDtypeStruct((C, wide), BF)
    mid_f = jax.ShapeDtypeStruct((C, n_pos), F32)

    both = jnp.concatenate([out_grad, inputs], axis=0).reshape(2 * C, n_pos)
    both = to_all(both, "ch", 16)
    pre = halo(pre_act.reshape(C, n_pos))
    w_two = weight_two.reshape(ROWS, CH)
    w_one = weight_one.reshape(ROWS, CH).T
    both, w_one, pre = lax.optimization_barrier((both, w_one, pre))

    own, over, pack = call(
        act_grad_body,
        (wide_f, wide_f, wide_f),
        [pltpu.VMEM((CH, n_pos), BF), pltpu.VMEM((3, 3 * C, wide), F32)],
        2,
    )(ids, w_two, both)
    pack = lax.ppermute(pack, LINE, to_side(0, True))

    send_two, keep_two = filter_sums(ids, *pre, both, True)
    send2 = send_two()
    pack, send2 = lax.optimization_barrier((pack, send2))
    got2 = lax.ppermute(send2, LINE, OTHER_CORE)
    own, oth, left, right = call(join_y_body, (wide_f, wide_f, mid_f, mid_f), [], 3)(
        ids, own, over, pack
    )
    from_left = lax.ppermute(right, LINE, to_side(1, False))
    from_right = lax.ppermute(left, LINE, to_side(-1, False))
    split2 = keep_two(got2)
    from_left, from_right, _ = lax.optimization_barrier((from_left, from_right, split2))
    delta = call(delta_body, (wide_b, wide_b), [], 6)(
        ids, own, oth, from_left, from_right, *pre
    )

    arrive2 = arrive(split2)
    send_one, keep_one = filter_sums(ids, *delta, both, False)
    got1 = lax.ppermute(send_one(), LINE, OTHER_CORE)
    split1 = keep_one(got1)
    arrive2, _ = lax.optimization_barrier((arrive2, split1))
    block2 = line_sum(arrive2, factor)
    delta, _ = lax.optimization_barrier((delta, block2))
    terms = call(
        data_body,
        jax.ShapeDtypeStruct((CH, n_pos), BF),
        [pltpu.VMEM((ROWS, n_pos), BF)],
        3,
    )(ids, *delta, w_one)
    got = lax.all_to_all(terms.reshape(16, C, n_pos), "ch", 0, 0, tiled=True)
    block1 = line_sum(arrive(split1), factor)
    spread2, spread1 = line_send(block2), line_send(block1)
    filter_two = write(ids, *line_join(spread2, (spread1[1], got)))
    input_grad = got.astype(F32).sum(axis=0).astype(BF).reshape(shape)
    filter_one = write(ids, *line_join(spread1, input_grad))
    return input_grad, filter_one, filter_two


def solution(mesh):
    field = P("ch", "sx", "sy", None)
    filt = P(None, "ch", None)
    return jax.shard_map(
        shards,
        mesh=mesh,
        in_specs=(field, field, field, filt, filt),
        out_specs=(field, filt, filt),
        check_vma=False,
    )
```

```python
import functools

import jax
import jax.numpy as jnp
from jax import lax
from jax.experimental import pallas as pl
from jax.experimental.pallas import tpu as pltpu
from jax.sharding import PartitionSpec as P

BF = jnp.bfloat16
F32 = jnp.float32
LINE = ("sx", "sy")
OFF = 27
OFFP = 28
C = 48
CH = 768
SLAB = 128
NXL = 4
ROWS = OFF * C
ROWSP = OFFP * C
HALF = CH // 2
BLOCK = ROWSP // 4


def place(chip, core):
    return ((chip % 2) * 2 + core) * 2 + chip // 2


OTHER_CORE = [(place(x, c), place(x, 1 - c)) for x in range(4) for c in range(2)]


def vmem():
    return pl.BlockSpec(memory_space=pltpu.VMEM)


def smem():
    return pl.BlockSpec(memory_space=pltpu.SMEM)


def call(body, outs, scratch, n_in, limit=16):
    return pl.pallas_call(
        body,
        out_shape=outs,
        in_specs=[smem()] + [vmem()] * n_in,
        out_specs=jax.tree.map(lambda _: vmem(), outs),
        scratch_shapes=scratch,
        compiler_params=pltpu.CompilerParams(vmem_limit_bytes=limit << 20),
    )


def lanes():
    return lax.broadcasted_iota(jnp.int32, (C, SLAB), 1)


def shift_z(part, c, lane):
    if c == 1:
        return part
    z = lane % 64
    if c == 0:
        return jnp.where(z >= 1, pltpu.roll(part, 1, 1), 0.0)
    return jnp.where(z <= 62, pltpu.roll(part, SLAB - 1, 1), 0.0)


def fill_windows(own_ref, oth_ref, stack_ref, sy, mirror, act):
    lane = lanes()
    low = lane < 64
    for xp in range(NXL + 2):
        at = slice(xp * SLAB, (xp + 1) * SLAB)
        own, oth = own_ref[:, at].astype(F32), oth_ref[:, at].astype(F32)
        if act:
            own, oth = jnp.maximum(own, 0.0), jnp.maximum(oth, 0.0)
        r_own, r_oth = pltpu.roll(own, 64, 1), pltpu.roll(oth, 64, 1)
        rows = (
            jnp.where(low, jnp.where(sy == 1, r_oth, 0.0), r_own),
            own,
            jnp.where(low, r_own, jnp.where(sy == 0, r_oth, 0.0)),
        )
        for b in range(3):
            for c in range(3):
                part = shift_z(rows[b], c, lane).astype(BF)
                for a in range(3):
                    xl = xp - a
                    if 0 <= xl < NXL:
                        o = 9 * a + 3 * b + c
                        o = 26 - o if mirror else o
                        stack_ref[o * C : (o + 1) * C, xl * SLAB : (xl + 1) * SLAB] = part


def nt(left, right):
    return lax.dot_general(left, right, (((1,), (1,)), ((), ())), preferred_element_type=F32)


def take(both_ref, second, field_ref):
    for k in range(16):
        field_ref[k * C : (k + 1) * C, :] = both_ref[k, second * C : (second + 1) * C, :]


def act_grad_body(ids, w_ref, both_ref, own_ref, over_ref, pack_ref, field_ref, u_ref):
    sy = ids[1]
    take(both_ref, 0, field_ref)
    grad = field_ref[...]
    u_ref[...] = jnp.zeros_like(u_ref)
    for a in range(3):
        for b in range(3):
            o = 9 * a + 3 * b
            y = jnp.dot(w_ref[o * C : (o + 3) * C, :], grad, preferred_element_type=F32)
            u_ref[b, :, a * SLAB : (a + NXL) * SLAB] += y
    lane = lanes()
    low = lane < 64
    for xp in range(NXL + 2):
        at = slice(xp * SLAB, (xp + 1) * SLAB)
        v = [
            sum(shift_z(u_ref[b, c * C : (c + 1) * C, at], 2 - c, lane) for c in range(3))
            for b in range(3)
        ]
        r0, r2 = pltpu.roll(v[0], 64, 1), pltpu.roll(v[2], 64, 1)
        own = v[1] + jnp.where(low, r0, r2)
        over = jnp.where(sy == 0, jnp.where(low, r2, 0.0), jnp.where(low, 0.0, r0))
        own_ref[:, at], over_ref[:, at] = own, over
        pack_ref[:, at] = jnp.where(low, jnp.where(sy == 0, over, own), jnp.where(sy == 0, own, over))


def join_y_body(ids, own_ref, over_ref, pack_ref, own_out, oth_out, left_out, right_out):
    sy = ids[1]
    low = lanes() < 64
    for xp in range(NXL + 2):
        at = slice(xp * SLAB, (xp + 1) * SLAB)
        pack = pack_ref[:, at]
        lower, upper = jnp.where(low, pack, 0.0), jnp.where(low, 0.0, pack)
        own = own_ref[:, at] + jnp.where(sy == 0, upper, lower)
        oth = over_ref[:, at] + jnp.where(sy == 0, lower, upper)
        own_out[:, at], oth_out[:, at] = own, oth
        for out, first in ((left_out, 0), (right_out, NXL)):
            if first <= xp < first + 2:
                k = (xp - first) * SLAB
                out[:, k : k + SLAB] = own
                out[:, k + 2 * SLAB : k + 3 * SLAB] = oth


def delta_body(ids, own_ref, oth_ref, left_ref, right_ref, pre_own_ref, pre_oth_ref, own_out, oth_out):
    for xp in range(NXL + 2):
        at = slice(xp * SLAB, (xp + 1) * SLAB)
        for grad_ref, pre_ref, out, half in (
            (own_ref, pre_own_ref, own_out, 0),
            (oth_ref, pre_oth_ref, oth_out, 2 * SLAB),
        ):
            grad = grad_ref[:, at]
            if xp < 2:
                k = half + xp * SLAB
                grad = grad + left_ref[:, k : k + SLAB]
            if xp >= NXL:
                k = half + (xp - NXL) * SLAB
                grad = grad + right_ref[:, k : k + SLAB]
            out[:, at] = jnp.where(pre_ref[:, at].astype(F32) > 0, grad, 0.0).astype(BF)


def send_body(act, ids, own_ref, oth_ref, both_ref, send_ref, stack_ref, full_ref):
    sy, core = ids[1], ids[2]
    take(both_ref, 0 if act else 1, full_ref)
    fill_windows(own_ref, oth_ref, stack_ref, sy, not act, act)
    other = full_ref[pl.ds(pl.multiple_of((1 - core) * HALF, HALF), HALF), :]
    for i in range(9):
        at = slice(i * 3 * C, (i + 1) * 3 * C)
        send_ref[at, :] = nt(stack_ref[at, :], other).astype(BF)
    send_ref[ROWS:ROWSP, :] = jnp.zeros((ROWSP - ROWS, HALF), BF)


def keep_body(act, ids, own_ref, oth_ref, both_ref, got_ref, keep_ref, *refs):
    send_refs, (stack_ref, full_ref) = refs[:3], refs[3:]
    sy, core, chip = ids[1], ids[2], ids[3]
    take(both_ref, 0 if act else 1, full_ref)
    fill_windows(own_ref, oth_ref, stack_ref, sy, not act, act)
    stack_ref[ROWS:ROWSP, :] = jnp.zeros((ROWSP - ROWS, NXL * SLAB), BF)
    mine = full_ref[pl.ds(pl.multiple_of(core * HALF, HALF), HALF), :]
    for k in (1, 3, 2, 0):
        for part in range(2):
            n = BLOCK // 2 - 8 * (1 - 2 * part)
            first = part * 160
            at = pl.ds(pl.multiple_of(((chip + k) % 4) * BLOCK + first, 16), n)
            total = nt(stack_ref[at, :], mine) + got_ref[at, :].astype(F32)
            to = slice(first, first + n)
            if k == 0:
                keep_ref[to, :] = total
            else:
                send_refs[k - 1][to, :] = total.astype(BF)


def data_body(ids, *refs):
    own_ref, oth_ref, w_ref, out_ref, stack_ref = refs
    fill_windows(own_ref, oth_ref, stack_ref, ids[1], True, False)
    for i in range(3):
        out_ref[i * 256 : (i + 1) * 256, :] = jnp.dot(
            w_ref[i * 256 : (i + 1) * 256, :], stack_ref[...], preferred_element_type=F32
        ).astype(BF)


def to_side(dx, flip):
    return [
        (sx * 2 + sy, (sx + dx) * 2 + (1 - sy if flip else sy))
        for sx in range(4)
        for sy in range(2)
        if 0 <= sx + dx < 4
    ]


def halo(whole):
    send = functools.partial(lax.ppermute, axis_name=LINE)
    first, last = whole[:, :SLAB], whole[:, whole.shape[1] - SLAB :]
    sides = []
    for flip, mid in ((False, whole), (True, send(whole, perm=to_side(0, True)))):
        left = send(last, perm=to_side(1, flip))
        right = send(first, perm=to_side(-1, flip))
        sides.append(jnp.concatenate([left, mid, right], axis=1))
    return tuple(sides)


def to_all(x, axis, count):
    many = jnp.broadcast_to(x[None], (count,) + x.shape)
    return lax.all_to_all(many, axis, 0, 0, tiled=True)


def along(shift):
    return [(place(x, c), place((x + shift) % 4, c)) for x in range(4) for c in range(2)]


def filter_sums(ids, own, oth, both, act):
    n_pos = NXL * SLAB
    field = pltpu.VMEM((CH, n_pos), BF)
    sent = jax.ShapeDtypeStruct((ROWSP, HALF), BF)
    outs = [jax.ShapeDtypeStruct((BLOCK, HALF), F32)]
    outs += [jax.ShapeDtypeStruct((BLOCK, HALF), BF)] * 3

    def send():
        scratch = [pltpu.VMEM((ROWS, n_pos), BF), field]
        return call(functools.partial(send_body, act), sent, scratch, 3)(ids, own, oth, both)

    def keep(got):
        scratch = [pltpu.VMEM((ROWSP, n_pos), BF), field]
        body = functools.partial(keep_body, act)
        return call(body, tuple(outs), scratch, 4)(ids, own, oth, both, got)

    return send, keep


def arrive(split):
    own, one, two, three = split
    return [own] + [lax.ppermute(v, LINE, along(k)) for k, v in ((1, one), (3, three), (2, two))]


def line_sum(parts, factor, after=None):
    if after is not None:
        parts, _ = lax.optimization_barrier((parts, after))
    total = parts[0]
    for v in parts[1:]:
        total = total + v.astype(F32)
    return (total * factor).astype(BF)


def line_send(block):
    return [block] + [lax.ppermute(block, LINE, along(k)) for k in (1, 3, 2)]


def line_join(parts, after):
    (own, one, three, two), _ = lax.optimization_barrier((parts, after))
    mine = jnp.concatenate([own, one, two, three], axis=0)
    return mine, lax.ppermute(mine, LINE, OTHER_CORE)


def write_body(ids, mine_ref, other_ref, out_ref):
    core = ids[2]
    for ref, half in ((mine_ref, core), (other_ref, 1 - core)):
        at = pl.ds(pl.multiple_of(half * HALF, HALF), HALF)
        out_ref[:, :, at] = ref[0].astype(F32)


def write(ids, mine, other):
    shape = (4, OFFP // 4, C, HALF)
    spec = pl.BlockSpec((1,) + shape[1:], lambda i, ids: ((ids[3] + 4 - i) % 4, 0, 0, 0))
    return pl.pallas_call(
        write_body,
        out_shape=jax.ShapeDtypeStruct((OFF, C, CH), F32),
        grid_spec=pltpu.PrefetchScalarGridSpec(
            num_scalar_prefetch=1,
            grid=(4,),
            in_specs=[spec, spec],
            out_specs=pl.BlockSpec((OFFP // 4, C, CH), lambda i, ids: (i, 0, 0)),
        ),
        compiler_params=pltpu.CompilerParams(vmem_limit_bytes=32 << 20),
    )(ids, mine.reshape(shape), other.reshape(shape))


def shards(inputs, pre_act, out_grad, weight_one, weight_two):
    shape = pre_act.shape
    sx, sy = lax.axis_index("sx"), lax.axis_index("sy")
    core = sx % 2
    chip = sx // 2 + 2 * sy
    ids = jnp.stack([sx, sy, core, chip]).astype(jnp.int32)
    n_pos = NXL * SLAB
    factor = 1.0 / 64.0
    wide = n_pos + 2 * SLAB
    wide_f = jax.ShapeDtypeStruct((C, wide), F32)
    wide_b = jax.ShapeDtypeStruct((C, wide), BF)
    mid_f = jax.ShapeDtypeStruct((C, n_pos), F32)

    both = jnp.concatenate([out_grad, inputs], axis=0).reshape(2 * C, n_pos)
    both = to_all(both, "ch", 16)
    pre = halo(pre_act.reshape(C, n_pos))
    w_two = weight_two.reshape(ROWS, CH)
    w_one = weight_one.reshape(ROWS, CH).T
    both, w_one, pre = lax.optimization_barrier((both, w_one, pre))

    own, over, pack = call(
        act_grad_body,
        (wide_f, wide_f, wide_f),
        [pltpu.VMEM((CH, n_pos), BF), pltpu.VMEM((3, 3 * C, wide), F32)],
        2,
    )(ids, w_two, both)
    pack = lax.ppermute(pack, LINE, to_side(0, True))

    send_two, keep_two = filter_sums(ids, *pre, both, True)
    send2 = send_two()
    pack, send2 = lax.optimization_barrier((pack, send2))
    got2 = lax.ppermute(send2, LINE, OTHER_CORE)
    own, oth, left, right = call(join_y_body, (wide_f, wide_f, mid_f, mid_f), [], 3)(
        ids, own, over, pack
    )
    from_left = lax.ppermute(right, LINE, to_side(1, False))
    from_right = lax.ppermute(left, LINE, to_side(-1, False))
    split2 = keep_two(got2)
    from_left, from_right, _ = lax.optimization_barrier((from_left, from_right, split2))
    delta = call(delta_body, (wide_b, wide_b), [], 6)(
        ids, own, oth, from_left, from_right, *pre
    )

    arrive2 = arrive(split2)
    send_one, keep_one = filter_sums(ids, *delta, both, False)
    got1 = lax.ppermute(send_one(), LINE, OTHER_CORE)
    split1 = keep_one(got1)
    delta, _ = lax.optimization_barrier((delta, split1))
    terms = call(
        data_body,
        jax.ShapeDtypeStruct((CH, n_pos), BF),
        [pltpu.VMEM((ROWS, n_pos), BF)],
        3,
    )(ids, *delta, w_one)
    arrive2, _ = lax.optimization_barrier((arrive2, (split1, terms)))
    block2 = line_sum(arrive2, factor)
    got = lax.all_to_all(terms.reshape(16, C, n_pos), "ch", 0, 0, tiled=True)
    block1 = line_sum(arrive(split1), factor)
    spread2, spread1 = line_send(block2), line_send(block1)
    filter_two = write(ids, *line_join(spread2, (spread1[1], got)))
    input_grad = got.astype(F32).sum(axis=0).astype(BF).reshape(shape)
    filter_one = write(ids, *line_join(spread1, input_grad))
    return input_grad, filter_one, filter_two


def solution(mesh):
    field = P("ch", "sx", "sy", None)
    filt = P(None, "ch", None)
    return jax.shard_map(
        shards,
        mesh=mesh,
        in_specs=(field, field, field, filt, filt),
        out_specs=(field, filt, filt),
        check_vma=False,
    )
```
